32 devices in a mesh: gx: 4 (over z), gy: 2 (over x), gz: 4 (over y, core).
Axes of the slice: x: 2, y: 2, z: 4, core: 2. Of those that a mesh axis runs over, the one named last changes fastest.
Arguments:
- density_start: float32 [64, 32, 512], P('gx', 'gy', 'gz'), may hold values from 0.7 to 1.3
- velocity_start: float32 [3, 64, 32, 512], P(None, 'gx', 'gy', 'gz'), may hold values from -0.75 to 0.75
- temp_start: float32 [64, 32, 512], P('gx', 'gy', 'gz'), may hold values from -6 to 6
- block_level: int32 [4, 2, 32], P('gx', 'gy', 'gz'), may hold values from 0 to 1
- solid_source: float32 [32, 32, 512], P('gx', 'gy', 'gz'), may hold values from -6 to 6
- ambient: float32 [32, 32, 512], P('gx', 'gy', 'gz'), may hold values from 0.5 to 2
- conduct: float32 [32, 32, 512], P('gx', 'gy', 'gz'), may hold values from 1 to 10
- pair_cell: int32 [32768], P(('gx', 'gy', 'gz')), may hold values from 0 to 32767
- pair_dest: int32 [32768, 1], P(('gx', 'gy', 'gz')), may hold values from 0 to 7; in each aligned block of 1024 rows (0 to 1023, 1024 to 2047, ...) at most 256 rows name the same one
- pair_solid: int32 [32768], P(('gx', 'gy', 'gz')), may hold values from 0 to 16383
- pair_coef: float32 [32768], P(('gx', 'gy', 'gz')), may hold values from 0.5 to 2
Outputs:
- fluid_temp: float32 [64, 32, 512], P('gx', 'gy', 'gz')
- fluid_vel: float32 [3, 64, 32, 512], P(None, 'gx', 'gy', 'gz')
- solid_temp: float32 [32, 32, 512], P('gx', 'gy', 'gz')
- wall_flux: float32 [64, 32, 512], P('gx', 'gy', 'gz')
The draws below stay inside these ranges and needn't reach their ends.
Inputs may be any that keep to these rules, and one draw needn't show every extreme that they name: `pair_dest`: among the 1024 pairs listed on one device, at most 256 name the same solid device, and some solid device is named exactly 256 times.
All inputs are finite; a program needn't handle non-finite values.
Results may differ from the reference program's by a relative error of at most 0.0001.
Values sent between devices are 32-bit elements; how exact they have to be, the bound alone decides.
A program may use at most 64 MiB of HBM per device.

```python
import math
import jax
import jax.numpy as jnp
import numpy as np

BLK = 16
FX = 16
FY = 16
FZ = 128
SX = 8
SY = 16
SZ = 128
PAIRS = 1024
ITERS = 2
NX = 64
NY = 32
NZ = 512
MX = 32
MY = 32
MZ = 512
TOTAL_PAIRS = 32768
N_GY = 2
N_GZ = 4


def place_ends(values, own_key, smallest, high):
    index_at = [jax.random.randint(jax.random.fold_in(own_key, axis), (), 0, length) for axis, length in enumerate(values.shape)]
    longest = values.shape.index(max(values.shape))
    next_to = index_at[:longest] + [(index_at[longest] + 1) % values.shape[longest]] + index_at[longest + 1:]
    return values.at[tuple(index_at)].set(smallest).at[tuple(next_to)].set(high)


def level_of(key, shape, shards, smallest, top_value):
    loudness, own = 1.0, jax.random.fold_in(key, 6)
    for axis_at, parts in shards:
        steps = jnp.exp(jax.random.uniform(jax.random.fold_in(own, axis_at), (parts,), jnp.float32, smallest / len(shards), top_value / len(shards)))
        loudness = loudness * jnp.repeat(steps, shape[axis_at] // parts).reshape([-1 if axis == axis_at else 1 for axis in range(len(shape))])
    return loudness


def shared_out(rng, own, number, rows, amount, top, reach, slope):
    ranking = jax.random.permutation(rng, amount)
    crowded, ordinary = portions_of(amount, rows * top, reach, slope, True), portions_of(amount, rows * top, reach, slope, False)
    places = jnp.arange(amount)

    def named(sizes, rotation):
        used = int((sizes > 0).sum())
        fixed = max(1, used // 4)
        passed = fixed + (places - fixed + rotation * (used - fixed)) % max(1, amount - fixed)
        return jnp.zeros((amount,), jnp.int32).at[ranking[jnp.where(places < fixed, places, passed)]].set(jnp.asarray(sizes, jnp.int32))

    sizes = jnp.where(number % 4 == 0, named(crowded, number // 4), named(ordinary, number - number // 4 - 1))
    mixed = jax.random.permutation(jax.random.fold_in(own, 3), amount)
    donor, receiver = mixed[0:amount // 2 * 2:2], mixed[1:amount // 2 * 2:2]
    slack = jnp.minimum(sizes[donor] - 1, reach - sizes[receiver]) // 2
    slack = jnp.where((donor == ranking[0]) | (receiver == ranking[0]) | (sizes[receiver] == 0), 0, jnp.maximum(slack, 0))
    passed = jax.random.randint(jax.random.fold_in(own, 4), (amount // 2,), 0, 1 << 20) % (slack + 1)
    sizes = sizes.at[donor].add(-passed).at[receiver].add(passed)
    labels = jnp.searchsorted(jnp.cumsum(sizes), jnp.arange(rows * top), side="right").astype(jnp.int32)
    table = labels.reshape(top, rows).T
    table = table[jax.random.permutation(jax.random.fold_in(own, 1), rows)]
    rotation = jax.random.randint(jax.random.fold_in(own, 2), (rows, 1), 0, top)
    return jnp.take_along_axis(table, (jnp.arange(top)[None, :] + rotation) % top, axis=1)


def portions_of(count, total, bound, skew, full):
    loads = [(1 << 20) // math.isqrt(standing ** skew) + 1 for standing in range(1, count + 1)]
    largest = bound if full else min(bound, max(-(-total // count), total * loads[0] // sum(loads)))
    least = 1 if total - largest >= count - 1 else 0
    given, surplus = [largest] + [least] * (count - 1), total - largest - least * (count - 1)
    while surplus > 0:
        movable = [i for i in range(1, count) if given[i] < largest] or [i for i in range(1, count) if given[i] < bound]
        mass, budget = sum([loads[i] for i in movable]), surplus
        for i in movable:
            extra = min(bound - given[i], max(1, budget * loads[i] // mass), surplus)
            given[i] = given[i] + extra
            surplus = surplus - extra
    return np.array(given)


def normal_values(key, extent, spread, reach, cuts=(), held_as=jnp.bfloat16):
    result = spread * jax.random.normal(key, extent, jnp.float32)
    if cuts:
        result = result * level_of(key, extent, cuts, -0.22, 0.18)
    return jnp.clip(result, -reach, reach).astype(held_as)


def setup_inputs(seed: int = 0) -> dict:
    key_of = jax.random.split(jax.random.key(seed), 12)
    density_start = jnp.clip(0.7 + 0.59999996 * jax.random.uniform(key_of[0], (NX, NY, NZ), jnp.float32) ** level_of(key_of[0], (NX, NY, NZ), ((0, 4), (1, 2), (2, 4)), -0.2, 0.2), 0.7, 1.3)
    velocity_start = normal_values(key_of[1], (3, NX, NY, NZ), 0.05, 0.75, ((1, 4), (2, 2), (3, 4)), jnp.float32)
    temp_start = normal_values(key_of[2], (NX, NY, NZ), 1.0, 6.0, ((0, 4), (1, 2), (2, 4)), jnp.float32)
    block_level = place_ends(jax.random.randint(key_of[3], (NX // BLK, NY // BLK, NZ // BLK), 0, 2), jax.random.fold_in(key_of[3], 1), 0, 1).astype(jnp.int32)
    solid_source = normal_values(key_of[4], (MX, MY, MZ), 1.0, 6.0, ((0, 4), (1, 2), (2, 4)), jnp.float32)
    ambient = jnp.clip(jnp.exp(math.log(2.0) - 1.3862944 * jax.random.uniform(key_of[5], (MX, MY, MZ), jnp.float32) ** level_of(key_of[5], (MX, MY, MZ), ((0, 4), (1, 2), (2, 4)), -0.2, 0.2)), 0.5, 2.0)
    conduct = jnp.clip(jnp.exp(math.log(10.0) - 2.3025851 * jax.random.uniform(key_of[6], (MX, MY, MZ), jnp.float32) ** level_of(key_of[6], (MX, MY, MZ), ((0, 4), (1, 2), (2, 4)), -0.2, 0.2)), 1.0, 10.0)
    pair_cell = place_ends(jax.random.randint(key_of[7], (TOTAL_PAIRS,), 0, FX * FY * FZ), jax.random.fold_in(key_of[7], 1), 0, (FX * FY * FZ) - 1).astype(jnp.int32)
    pair_dest_keys = jax.random.split(jax.random.fold_in(key_of[8], 1), TOTAL_PAIRS // PAIRS)
    pair_dest_turns = jax.random.permutation(jax.random.fold_in(key_of[8], 3), TOTAL_PAIRS // PAIRS)
    pair_dest = jax.vmap(lambda own, number: shared_out(jax.random.fold_in(key_of[8], 2), own, number, PAIRS, N_GY * N_GZ, 1, 2 * PAIRS // (N_GY * N_GZ), 1))(pair_dest_keys, pair_dest_turns).reshape((TOTAL_PAIRS, 1))
    pair_solid = place_ends(jax.random.randint(key_of[9], (TOTAL_PAIRS,), 0, SX * SY * SZ), jax.random.fold_in(key_of[9], 1), 0, (SX * SY * SZ) - 1).astype(jnp.int32)
    pair_coef = jnp.clip(jnp.exp(math.log(2.0) - 1.3862944 * jax.random.uniform(key_of[10], (TOTAL_PAIRS,), jnp.float32) ** level_of(key_of[10], (TOTAL_PAIRS,), ((0, 32),), -0.2, 0.2)), 0.5, 2.0)
    return dict(density_start=density_start, velocity_start=velocity_start, temp_start=temp_start, block_level=block_level, solid_source=solid_source, ambient=ambient, conduct=conduct, pair_cell=pair_cell, pair_dest=pair_dest, pair_solid=pair_solid, pair_coef=pair_coef)


velocity_set = ((0, 0, 0), (1, 0, 0), (-1, 0, 0), (0, 1, 0), (0, -1, 0), (0, 0, 1), (0, 0, -1),
                (1, 1, 0), (-1, -1, 0), (1, -1, 0), (-1, 1, 0), (1, 0, 1), (-1, 0, -1), (1, 0, -1),
                (-1, 0, 1), (0, 1, 1), (0, -1, -1), (0, 1, -1), (0, -1, 1))
weight_flow = (1.0 / 3.0,) + (1.0 / 18.0,) * 6 + (1.0 / 36.0,) * 12
weight_heat = (0.25,) + (0.125,) * 6


def projection(which, speed):
    along = jnp.zeros_like(speed[0])
    for dimen in range(3):
        sign = velocity_set[which][dimen]
        if sign == 1:
            along = along + speed[dimen]
        elif sign == -1:
            along = along - speed[dimen]
    return along


def moments(flow):
    density = flow[0]
    for which in range(1, 19):
        density = density + flow[which]
    speed = []
    for dimen in range(3):
        total = jnp.zeros_like(density)
        for which in range(19):
            sign = velocity_set[which][dimen]
            if sign == 1:
                total = total + flow[which]
            elif sign == -1:
                total = total - flow[which]
        speed.append(total / density)
    return density, speed


def flow_balance(density, speed):
    square = speed[0] * speed[0] + speed[1] * speed[1] + speed[2] * speed[2]
    rows_out = []
    for which in range(19):
        along = projection(which, speed)
        rows_out.append(weight_flow[which] * density * (1.0 + 3.0 * along + 4.5 * along * along - 1.5 * square))
    return jnp.stack(rows_out)


def heat_balance(temper, speed):
    rows_out = []
    for which in range(7):
        along = projection(which, speed)
        rows_out.append(weight_heat[which] * temper * (1.0 + 4.0 * along))
    return jnp.stack(rows_out)


def relax(flow, heat, fine, every):
    density, speed = moments(flow)
    temper = jnp.sum(heat, axis=0)
    rate_flow = jnp.where(fine, 1.0 / 1.3, 1.0 / 0.9)
    rate_heat = jnp.where(fine, 1.0 / 1.1, 1.0 / 0.8)
    new_flow = flow - rate_flow * (flow - flow_balance(density, speed))
    new_heat = heat - rate_heat * (heat - heat_balance(temper, speed))
    if not every:
        new_flow = jnp.where(fine, new_flow, flow)
        new_heat = jnp.where(fine, new_heat, heat)
    return new_flow, new_heat


def neighbours(padded):
    return (padded[2:, 1:-1, 1:-1], padded[:-2, 1:-1, 1:-1], padded[1:-1, 2:, 1:-1],
            padded[1:-1, :-2, 1:-1], padded[1:-1, 1:-1, 2:], padded[1:-1, 1:-1, :-2])


def face_weights(conduct, padded):
    return [2.0 * conduct * other / (conduct + other) for other in neighbours(padded)]


def apply_operator(field, padded, diagonal, weights):
    total = diagonal * field
    for weight, other in zip(weights, neighbours(padded)):
        total = total + weight * (field - other)
    return total


def reference(density_start, velocity_start, temp_start, block_level, solid_source, ambient, conduct,
              pair_cell, pair_dest, pair_solid, pair_coef):
    fine = jnp.repeat(jnp.repeat(jnp.repeat(block_level == 1, BLK, 0), BLK, 1), BLK, 2)
    speed0 = [velocity_start[0], velocity_start[1], velocity_start[2]]
    flow = flow_balance(density_start, speed0)
    heat = heat_balance(temp_start, speed0)
    for substep in range(2):
        flow, heat = relax(flow, heat, fine, substep == 0)
        flow = jnp.stack([jnp.roll(flow[which], velocity_set[which], axis=(0, 1, 2)) for which in range(19)])
        heat = jnp.stack([jnp.roll(heat[which], velocity_set[which], axis=(0, 1, 2)) for which in range(7)])
    density, speed = moments(flow)
    fluid_temp = jnp.sum(heat, axis=0)
    fluid_vel = jnp.stack(speed)

    source_dev = jnp.arange(TOTAL_PAIRS, dtype=jnp.int32) // PAIRS
    dev_x = source_dev // (N_GY * N_GZ)
    dev_y = (source_dev // N_GZ) % N_GY
    dev_z = source_dev % N_GZ
    cell_x = pair_cell // (FY * FZ)
    cell_y = (pair_cell // FZ) % FY
    cell_z = pair_cell % FZ
    fluid_flat = ((dev_x * FX + cell_x) * NY + dev_y * FY + cell_y) * NZ + dev_z * FZ + cell_z
    dest = pair_dest[:, 0]
    dest_y = dest // N_GZ
    dest_z = dest % N_GZ
    sol_x = pair_solid // (SY * SZ)
    sol_y = (pair_solid // SZ) % SY
    sol_z = pair_solid % SZ
    solid_flat = ((dev_x * SX + sol_x) * MY + dest_y * SY + sol_y) * MZ + dest_z * SZ + sol_z
    fluid_flat = fluid_flat.astype(jnp.int32)
    solid_flat = solid_flat.astype(jnp.int32)

    temp_at = fluid_temp.reshape(-1)[fluid_flat]
    zeros_solid = jnp.zeros((MX * MY * MZ,), dtype=fluid_temp.dtype)
    gain = zeros_solid.at[solid_flat].add(pair_coef).reshape(MX, MY, MZ)
    inflow = zeros_solid.at[solid_flat].add(pair_coef * temp_at).reshape(MX, MY, MZ)
    load = solid_source + inflow

    weights = face_weights(conduct, jnp.pad(conduct, 1))
    diagonal = ambient + gain
    solid_temp = jnp.zeros_like(load)
    residual, direction = load, load
    norm_now = jnp.sum(residual * residual)
    for step in range(ITERS):
        image = apply_operator(direction, jnp.pad(direction, 1), diagonal, weights)
        alpha = norm_now / jnp.sum(direction * image)
        solid_temp = solid_temp + alpha * direction
        residual = residual - alpha * image
        norm_next = jnp.sum(residual * residual)
        direction = residual + (norm_next / norm_now) * direction
        norm_now = norm_next

    wall_at = solid_temp.reshape(-1)[solid_flat]
    flux = pair_coef * (wall_at - temp_at)
    wall_flux = jnp.zeros((NX * NY * NZ,), dtype=fluid_temp.dtype).at[fluid_flat].add(flux).reshape(NX, NY, NZ)
    return fluid_temp, fluid_vel, solid_temp, wall_flux
```

```python
import functools

import jax
import jax.numpy as jnp
from jax import lax
from jax.experimental import pallas as pl
from jax.experimental.pallas import tpu as pltpu
from jax.sharding import PartitionSpec as P

BLK = 16
ITERS = 2


velocity_set = (
    (0, 0, 0),
    (1, 0, 0),
    (-1, 0, 0),
    (0, 1, 0),
    (0, -1, 0),
    (0, 0, 1),
    (0, 0, -1),
    (1, 1, 0),
    (-1, -1, 0),
    (1, -1, 0),
    (-1, 1, 0),
    (1, 0, 1),
    (-1, 0, -1),
    (1, 0, -1),
    (-1, 0, 1),
    (0, 1, 1),
    (0, -1, -1),
    (0, 1, -1),
    (0, -1, 1),
)
weight_flow = (1.0 / 3.0,) + (1.0 / 18.0,) * 6 + (1.0 / 36.0,) * 12
weight_heat = (0.25,) + (0.125,) * 6
stacked_set = velocity_set + velocity_set[:7]


def with_halo(cells, sides, width, closed):
    for axis, dim in sides:
        count = lax.axis_size(axis)
        ends = count if closed else count - 1
        head = lax.slice_in_dim(cells, 0, width, axis=dim)
        tail = lax.slice_in_dim(cells, cells.shape[dim] - width, cells.shape[dim], axis=dim)
        cells = jnp.concatenate(
            [
                lax.ppermute(tail, axis, [(i, (i + 1) % count) for i in range(ends)]),
                cells,
                lax.ppermute(head, axis, [((i + 1) % count, i) for i in range(ends)]),
            ],
            axis=dim,
        )
    return cells

AXES = ("gx", "gy", "gz")
HALO = 2
VMEM = pltpu.VMEM


def ring_halo(cells, axis, dim, total):
    count = lax.axis_size(axis)
    size = cells.shape[dim]
    head = lax.slice_in_dim(cells, 0, HALO, axis=dim)
    tail = lax.slice_in_dim(cells, size - HALO, size, axis=dim)
    after = lax.ppermute(head, axis, [((i + 1) % count, i) for i in range(count)])
    before = lax.ppermute(tail, axis, [(i, (i + 1) % count) for i in range(count)])
    gap = list(cells.shape)
    gap[dim] = total - size - 2 * HALO
    return jnp.concatenate([cells, after, jnp.ones(gap, cells.dtype), before], axis=dim)


def along_of(which, speed):
    along = None
    for dimen in range(3):
        sign = velocity_set[which][dimen]
        if sign == 1:
            along = speed[dimen] if along is None else along + speed[dimen]
        elif sign == -1:
            along = -speed[dimen] if along is None else along - speed[dimen]
    return along


def equilibrium(density, speed):
    square = 1.0 - 1.5 * (speed[0] * speed[0] + speed[1] * speed[1] + speed[2] * speed[2])
    weighted = {w: w * density for w in set(weight_flow)}
    rows_out = [weighted[weight_flow[0]] * square]
    for which in range(1, 19, 2):
        along = along_of(which, speed)
        rho = weighted[weight_flow[which]]
        even = rho * (square + 4.5 * along * along)
        odd = rho * (3.0 * along)
        rows_out += [even + odd, even - odd]
    return rows_out


def heat_equilibrium(temper, speed):
    rows_out = [weight_heat[0] * temper]
    for which in range(1, 7, 2):
        even = weight_heat[which] * temper
        odd = even * (4.0 * along_of(which, speed))
        rows_out += [even + odd, even - odd]
    return rows_out


def flow_moments(flow):
    density = flow[0]
    for which in range(1, 19):
        density = density + flow[which]
    inverse = 1.0 / density
    speed = []
    for dimen in range(3):
        total = None
        for which in range(19):
            sign = velocity_set[which][dimen]
            if sign == 1:
                total = flow[which] if total is None else total + flow[which]
            elif sign == -1:
                total = total - flow[which]
        speed.append(total * inverse)
    return density, speed


def collide(flow, heat, rate_flow, rate_heat):
    density, speed = flow_moments(flow)
    temper = functools.reduce(lambda a, b: a + b, heat)
    flow = [f - rate_flow * (f - e) for f, e in zip(flow, equilibrium(density, speed))]
    heat = [g - rate_heat * (g - e) for g, e in zip(heat, heat_equilibrium(temper, speed))]
    return flow, heat


def stream_plane(store, plane, values):
    height, width = values[0].shape
    for which, value in enumerate(values):
        off_x, off_y, off_z = stacked_set[which]
        if off_y:
            value = pltpu.roll(value, off_y % height, 0)
        if off_z:
            value = pltpu.roll(value, off_z % width, 1)
        store[which, plane + off_x + 1] = value


def fluid_kernel(fields, temp_out, vel_out, first, second):
    planes = fields.shape[1]
    size_x, size_y, size_z = temp_out.shape

    def one(plane, carry):
        density = fields[0, plane]
        speed = [fields[1, plane], fields[2, plane], fields[3, plane]]
        fine = fields[5, plane] == 1.0
        flow, heat = collide(
            equilibrium(density, speed),
            heat_equilibrium(fields[4, plane], speed),
            jnp.where(fine, 1.0 / 1.3, 1.0 / 0.9),
            jnp.where(fine, 1.0 / 1.1, 1.0 / 0.8),
        )
        stream_plane(first, plane, flow + heat)
        return carry

    def two(plane, carry):
        fine = fields[5, plane] == 1.0
        values = [first[which, plane + 1] for which in range(26)]
        flow, heat = collide(
            values[:19], values[19:], jnp.where(fine, 1.0 / 1.3, 0.0), jnp.where(fine, 1.0 / 1.1, 0.0)
        )
        stream_plane(second, plane, flow + heat)
        return carry

    def three(row, carry):
        plane = row + HALO + 1
        values = [second[which, plane, :size_y, :size_z] for which in range(26)]
        density, speed = flow_moments(values[:19])
        temp_out[row] = functools.reduce(lambda a, b: a + b, values[19:])
        for dimen in range(3):
            vel_out[dimen, row] = speed[dimen]
        return carry

    lax.fori_loop(0, planes, one, 0)
    lax.fori_loop(1, planes - 1, two, 0)
    lax.fori_loop(0, size_x, three, 0)


def run_fluid(fields, shape):
    planes, height, width = fields.shape[1:]
    whole = pl.BlockSpec(memory_space=VMEM)
    return pl.pallas_call(
        fluid_kernel,
        out_shape=(jax.ShapeDtypeStruct(shape, jnp.float32), jax.ShapeDtypeStruct((3,) + shape, jnp.float32)),
        in_specs=[whole],
        out_specs=(whole, whole),
        scratch_shapes=[VMEM((26, planes + 2, height, width), jnp.float32)] * 2,
        compiler_params=pltpu.CompilerParams(vmem_limit_bytes=52 * 1024 * 1024),
        name="fluid",
    )(fields)


def thirds(value):
    high = value.astype(jnp.bfloat16)
    rest = value - high.astype(jnp.float32)
    middle = rest.astype(jnp.bfloat16)
    low = (rest - middle.astype(jnp.float32)).astype(jnp.bfloat16)
    return [high, middle, low]


def one_hot(index, count):
    rows = lax.broadcasted_iota(jnp.int32, (count, index.shape[1]), 0)
    return rows == index


def take(table, index):
    rows, lanes = table.shape
    pick = one_hot(index // lanes, rows).astype(jnp.float32).astype(jnp.bfloat16)
    inside = one_hot(index % lanes, lanes)
    got = None
    for part in thirds(table):
        term = lax.dot_general(part, pick, (((0,), (0,)), ((), ())), preferred_element_type=jnp.float32)
        got = term if got is None else got + term
    return jnp.sum(jnp.where(inside, got, 0.0), axis=0, keepdims=True)


def put(values, index, rows, lanes):
    hot = one_hot(index // lanes, rows).astype(jnp.float32)
    inside = one_hot(index % lanes, lanes).astype(jnp.float32).astype(jnp.bfloat16)
    outs = []
    for value in values:
        total = None
        for part in thirds(value):
            left = (hot * part.astype(jnp.float32)).astype(jnp.bfloat16)
            term = lax.dot_general(left, inside, (((1,), (1,)), ((), ())), preferred_element_type=jnp.float32)
            total = term if total is None else total + term
        outs.append(total)
    return outs


def send_kernel(temp, cell, slot, coef, solid, temp_at, outgoing):
    lanes = temp.shape[1]
    got = take(temp[...], cell[...])
    temp_at[...] = got
    rows = outgoing.shape[1]
    filled = put([got, coef[...], solid[...]], slot[...], rows, lanes)
    for which in range(3):
        outgoing[which] = filled[which]


def land_kernel(arrived, source, gain, load):
    rows, lanes = source.shape
    temp, coef = arrived[0:1, :], arrived[1:2, :]
    cell = (arrived[2:3, :] + 0.5).astype(jnp.int32)
    total, inflow = put([coef, coef * temp], cell, rows, lanes)
    gain[...] = total
    load[...] = source[...] + inflow


def wall_kernel(solid, arrived, out):
    out[...] = take(solid[...], (arrived[2:3, :] + 0.5).astype(jnp.int32))


def flux_kernel(returned, slot, cell, coef, temp_at, out):
    rows, lanes = out.shape
    wall = take(returned[...], slot[...])
    out[...] = put([coef[...] * (wall - temp_at[...])], cell[...], rows, lanes)[0]


def local_call(kernel, outs, *args):
    whole = pl.BlockSpec(memory_space=VMEM)
    many = isinstance(outs[0], tuple)
    shaped = [jax.ShapeDtypeStruct(o, jnp.float32) for o in (outs if many else (outs,))]
    return pl.pallas_call(
        kernel,
        out_shape=tuple(shaped) if many else shaped[0],
        in_specs=[whole] * len(args),
        out_specs=(whole,) * len(shaped) if many else whole,
        name=kernel.__name__,
    )(*args)


def total_kernel(sizes, mine, out, held, send_sem, recv_sem):
    devices = sizes[0] * sizes[1] * sizes[2]
    me = (lax.axis_index("gx") * sizes[1] + lax.axis_index("gy")) * sizes[2] + lax.axis_index("gz")

    def place(step):
        other = lax.rem(me + step, devices)
        rest = lax.rem(other, sizes[1] * sizes[2])
        return (other // (sizes[1] * sizes[2]), rest // sizes[2], lax.rem(rest, sizes[2]))

    barrier = pltpu.get_barrier_semaphore()

    def greet(step, carry):
        pl.semaphore_signal(barrier, inc=1, device_id=place(step), device_id_type=pl.DeviceIdType.MESH)
        return carry

    def copy_of(step):
        return pltpu.make_async_remote_copy(
            src_ref=mine,
            dst_ref=held.at[step],
            send_sem=send_sem.at[step],
            recv_sem=recv_sem.at[step],
            device_id=place(step),
            device_id_type=pl.DeviceIdType.MESH,
        )

    def send(step, carry):
        copy_of(step).start()
        return carry

    def finish(step, carry):
        copy_of(step).wait()
        return carry

    lax.fori_loop(1, devices, greet, 0)
    pl.semaphore_wait(barrier, devices - 1)
    lax.fori_loop(1, devices, send, 0)
    lax.fori_loop(1, devices, finish, 0)
    out[...] = lax.fori_loop(1, devices, lambda step, total: total + held[step], mine[...])


def total_over_devices(values):
    sizes = tuple(lax.axis_size(axis) for axis in AXES)
    devices = sizes[0] * sizes[1] * sizes[2]
    whole = pl.BlockSpec(memory_space=VMEM)
    return pl.pallas_call(
        functools.partial(total_kernel, sizes),
        out_shape=jax.ShapeDtypeStruct(values.shape, values.dtype),
        in_specs=[whole],
        out_specs=whole,
        scratch_shapes=[
            VMEM((devices,) + values.shape, values.dtype),
            pltpu.SemaphoreType.DMA((devices,)),
            pltpu.SemaphoreType.DMA((devices,)),
        ],
        compiler_params=pltpu.CompilerParams(collective_id=0, has_side_effects=True),
        name="total",
    )(values)


def neighbours(padded):
    return (
        padded[2:, 1:-1, 1:-1],
        padded[:-2, 1:-1, 1:-1],
        padded[1:-1, 2:, 1:-1],
        padded[1:-1, :-2, 1:-1],
        padded[1:-1, 1:-1, 2:],
        padded[1:-1, 1:-1, :-2],
    )


def apply_operator(field, diagonal, weights):
    padded = with_halo(field, (("gx", 0), ("gy", 1), ("gz", 2)), 1, False)
    total = diagonal * field
    for weight, other in zip(weights, neighbours(padded)):
        total = total + weight * (field - other)
    return total


def per_device(
    density_start,
    velocity_start,
    temp_start,
    block_level,
    solid_source,
    ambient,
    conduct,
    pair_cell,
    pair_dest,
    pair_solid,
    pair_coef,
):
    size_x, size_y, size_z = density_start.shape
    blocks_x, blocks_y, blocks_z = block_level.shape
    fine = jnp.broadcast_to(
        (block_level == 1)[:, None, :, None, :, None], (blocks_x, BLK, blocks_y, BLK, blocks_z, BLK)
    ).reshape(size_x, size_y, size_z)
    fields = jnp.stack(
        [density_start, velocity_start[0], velocity_start[1], velocity_start[2], temp_start, fine.astype(jnp.float32)]
    )
    count = lax.axis_size("gx")
    fields = jnp.concatenate(
        [
            lax.ppermute(fields[:, -HALO:], "gx", [(i, (i + 1) % count) for i in range(count)]),
            fields,
            lax.ppermute(fields[:, :HALO], "gx", [((i + 1) % count, i) for i in range(count)]),
        ],
        axis=1,
    )
    fields = ring_halo(fields, "gy", 2, size_y + 8)
    fields = ring_halo(fields, "gz", 3, size_z + 128)
    fluid_temp, fluid_vel = run_fluid(fields, (size_x, size_y, size_z))

    groups = lax.axis_size(("gy", "gz"))
    pair_count = pair_cell.shape[0]
    capacity = 2 * pair_count // groups
    dest = pair_dest[:, 0]
    onehot = (dest[:, None] == jnp.arange(groups, dtype=jnp.int32)[None, :]).astype(jnp.int32)
    rank = jnp.sum((jnp.cumsum(onehot, axis=0) - onehot) * onehot, axis=1)
    slot = (dest * capacity + rank)[None, :]
    cell = pair_cell[None, :]
    coef = pair_coef[None, :]
    solid = pair_solid.astype(jnp.float32)[None, :]
    slot_rows = groups * capacity // size_z
    temp_at, outgoing = local_call(
        send_kernel,
        ((1, pair_count), (3, slot_rows, size_z)),
        fluid_temp.reshape(size_x * size_y, size_z), cell, slot, coef, solid,
    )
    arrived = lax.all_to_all(
        outgoing.reshape(3, groups, capacity), ("gy", "gz"), split_axis=1, concat_axis=1, tiled=True
    ).reshape(3, groups * capacity)
    solid_shape = solid_source.shape
    flat = (solid_shape[0] * solid_shape[1], solid_shape[2])
    gain, load = local_call(land_kernel, (flat, flat), arrived, solid_source.reshape(flat))
    diagonal = ambient + gain.reshape(solid_shape)
    residual = load.reshape(solid_shape)
    conduct_pad = with_halo(conduct, (("gx", 0), ("gy", 1), ("gz", 2)), 1, False)
    weights = [2.0 * conduct * other / (conduct + other) for other in neighbours(conduct_pad)]
    image = apply_operator(residual, diagonal, weights)
    twice = apply_operator(image, diagonal, weights)
    sums = [jnp.sum(a * b, axis=(0, 1)) for a, b in ((residual, residual), (residual, image), (image, image), (image, twice))]
    sums = total_over_devices(jnp.stack(sums + sums))
    sums = jnp.sum(sums, axis=1)
    norm, product, square, cross = sums[0], sums[1], sums[2], sums[3]
    alpha = norm / product
    norm_next = norm - 2.0 * alpha * product + alpha * alpha * square
    product_next = product - 2.0 * alpha * square + alpha * alpha * cross
    ratio = norm_next / norm
    alpha_next = norm_next / (product_next - ratio * norm_next / alpha)
    solid_temp = (alpha + alpha_next * (1.0 + ratio)) * residual - (alpha_next * alpha) * image

    wall = local_call(wall_kernel, (1, groups * capacity), solid_temp.reshape(flat), arrived)
    returned = lax.all_to_all(wall.reshape(groups, capacity), ("gy", "gz"), split_axis=0, concat_axis=0, tiled=True)
    wall_flux = local_call(
        flux_kernel, (size_x * size_y, size_z), returned.reshape(slot_rows, size_z), slot, cell, coef, temp_at
    )
    return (fluid_temp, fluid_vel, solid_temp, wall_flux.reshape(size_x, size_y, size_z))


def solution(mesh):
    return jax.shard_map(
        per_device,
        mesh=mesh,
        in_specs=(
            P("gx", "gy", "gz"),
            P(None, "gx", "gy", "gz"),
            P("gx", "gy", "gz"),
            P("gx", "gy", "gz"),
            P("gx", "gy", "gz"),
            P("gx", "gy", "gz"),
            P("gx", "gy", "gz"),
            P(("gx", "gy", "gz")),
            P(("gx", "gy", "gz"), None),
            P(("gx", "gy", "gz")),
            P(("gx", "gy", "gz")),
        ),
        out_specs=(
            P("gx", "gy", "gz"),
            P(None, "gx", "gy", "gz"),
            P("gx", "gy", "gz"),
            P("gx", "gy", "gz"),
        ),
        check_vma=False,
    )
```

```python
import functools

import jax
import jax.numpy as jnp
from jax import lax
from jax.experimental import pallas as pl
from jax.experimental.pallas import tpu as pltpu
from jax.sharding import PartitionSpec as P

BLK = 16
ITERS = 2


velocity_set = (
    (0, 0, 0),
    (1, 0, 0),
    (-1, 0, 0),
    (0, 1, 0),
    (0, -1, 0),
    (0, 0, 1),
    (0, 0, -1),
    (1, 1, 0),
    (-1, -1, 0),
    (1, -1, 0),
    (-1, 1, 0),
    (1, 0, 1),
    (-1, 0, -1),
    (1, 0, -1),
    (-1, 0, 1),
    (0, 1, 1),
    (0, -1, -1),
    (0, 1, -1),
    (0, -1, 1),
)
weight_flow = (1.0 / 3.0,) + (1.0 / 18.0,) * 6 + (1.0 / 36.0,) * 12
weight_heat = (0.25,) + (0.125,) * 6
stacked_set = velocity_set + velocity_set[:7]


AXES = ("gx", "gy", "gz")
HALO = 2
VMEM = pltpu.VMEM


def ring_halo(cells, axis, dim, total):
    count = lax.axis_size(axis)
    size = cells.shape[dim]
    head = lax.slice_in_dim(cells, 0, HALO, axis=dim)
    tail = lax.slice_in_dim(cells, size - HALO, size, axis=dim)
    after = lax.ppermute(head, axis, [((i + 1) % count, i) for i in range(count)])
    before = lax.ppermute(tail, axis, [(i, (i + 1) % count) for i in range(count)])
    gap = list(cells.shape)
    gap[dim] = total - size - 2 * HALO
    return jnp.concatenate([cells, after, jnp.ones(gap, cells.dtype), before], axis=dim)


def along_of(which, speed):
    along = None
    for dimen in range(3):
        sign = velocity_set[which][dimen]
        if sign == 1:
            along = speed[dimen] if along is None else along + speed[dimen]
        elif sign == -1:
            along = -speed[dimen] if along is None else along - speed[dimen]
    return along


def equilibrium(density, speed):
    square = 1.0 - 1.5 * (speed[0] * speed[0] + speed[1] * speed[1] + speed[2] * speed[2])
    weighted = {w: w * density for w in set(weight_flow)}
    rows_out = [weighted[weight_flow[0]] * square]
    for which in range(1, 19, 2):
        along = along_of(which, speed)
        rho = weighted[weight_flow[which]]
        even = rho * (square + 4.5 * along * along)
        odd = rho * (3.0 * along)
        rows_out += [even + odd, even - odd]
    return rows_out


def heat_equilibrium(temper, speed):
    rows_out = [weight_heat[0] * temper]
    for which in range(1, 7, 2):
        even = weight_heat[which] * temper
        odd = even * (4.0 * along_of(which, speed))
        rows_out += [even + odd, even - odd]
    return rows_out


def flow_moments(flow):
    density = flow[0]
    for which in range(1, 19):
        density = density + flow[which]
    inverse = 1.0 / density
    speed = []
    for dimen in range(3):
        total = None
        for which in range(19):
            sign = velocity_set[which][dimen]
            if sign == 1:
                total = flow[which] if total is None else total + flow[which]
            elif sign == -1:
                total = total - flow[which]
        speed.append(total * inverse)
    return density, speed


def collide(flow, heat, rate_flow, rate_heat):
    density, speed = flow_moments(flow)
    temper = functools.reduce(lambda a, b: a + b, heat)
    flow = [f - rate_flow * (f - e) for f, e in zip(flow, equilibrium(density, speed))]
    heat = [g - rate_heat * (g - e) for g, e in zip(heat, heat_equilibrium(temper, speed))]
    return flow, heat


def stream_plane(store, plane, values):
    height, width = values[0].shape
    for which, value in enumerate(values):
        off_x, off_y, off_z = stacked_set[which]
        if off_y:
            value = pltpu.roll(value, off_y % height, 0)
        if off_z:
            value = pltpu.roll(value, off_z % width, 1)
        store[which, plane + off_x + 1] = value


def fluid_kernel(fields, temp_out, vel_out, first, second):
    planes = fields.shape[1]
    size_x, size_y, size_z = temp_out.shape

    def one(plane, carry):
        density = fields[0, plane]
        speed = [fields[1, plane], fields[2, plane], fields[3, plane]]
        fine = fields[5, plane] == 1.0
        flow, heat = collide(
            equilibrium(density, speed),
            heat_equilibrium(fields[4, plane], speed),
            jnp.where(fine, 1.0 / 1.3, 1.0 / 0.9),
            jnp.where(fine, 1.0 / 1.1, 1.0 / 0.8),
        )
        stream_plane(first, plane, flow + heat)
        return carry

    def two(plane, carry):
        fine = fields[5, plane] == 1.0
        values = [first[which, plane + 1] for which in range(26)]
        flow, heat = collide(
            values[:19], values[19:], jnp.where(fine, 1.0 / 1.3, 0.0), jnp.where(fine, 1.0 / 1.1, 0.0)
        )
        stream_plane(second, plane, flow + heat)
        return carry

    def three(row, carry):
        plane = row + HALO + 1
        values = [second[which, plane, :size_y, :size_z] for which in range(26)]
        density, speed = flow_moments(values[:19])
        temp_out[row] = functools.reduce(lambda a, b: a + b, values[19:])
        for dimen in range(3):
            vel_out[dimen, row] = speed[dimen]
        return carry

    lax.fori_loop(0, planes, one, 0)
    lax.fori_loop(1, planes - 1, two, 0)
    lax.fori_loop(0, size_x, three, 0)


def run_fluid(fields, shape):
    planes, height, width = fields.shape[1:]
    whole = pl.BlockSpec(memory_space=VMEM)
    return pl.pallas_call(
        fluid_kernel,
        out_shape=(jax.ShapeDtypeStruct(shape, jnp.float32), jax.ShapeDtypeStruct((3,) + shape, jnp.float32)),
        in_specs=[whole],
        out_specs=(whole, whole),
        scratch_shapes=[VMEM((26, planes + 2, height, width), jnp.float32)] * 2,
        compiler_params=pltpu.CompilerParams(vmem_limit_bytes=52 * 1024 * 1024),
        name="fluid",
    )(fields)


def thirds(value):
    high = value.astype(jnp.bfloat16)
    rest = value - high.astype(jnp.float32)
    middle = rest.astype(jnp.bfloat16)
    low = (rest - middle.astype(jnp.float32)).astype(jnp.bfloat16)
    return [high, middle, low]


def one_hot(index, count):
    rows = lax.broadcasted_iota(jnp.int32, (count, index.shape[1]), 0)
    return rows == index


def take(table, index):
    rows, lanes = table.shape
    pick = one_hot(index // lanes, rows).astype(jnp.float32).astype(jnp.bfloat16)
    inside = one_hot(index % lanes, lanes)
    got = None
    for part in thirds(table):
        term = lax.dot_general(part, pick, (((0,), (0,)), ((), ())), preferred_element_type=jnp.float32)
        got = term if got is None else got + term
    return jnp.sum(jnp.where(inside, got, 0.0), axis=0, keepdims=True)


def put(values, index, rows, lanes):
    hot = one_hot(index // lanes, rows).astype(jnp.float32)
    inside = one_hot(index % lanes, lanes).astype(jnp.float32).astype(jnp.bfloat16)
    outs = []
    for value in values:
        total = None
        for part in thirds(value):
            left = (hot * part.astype(jnp.float32)).astype(jnp.bfloat16)
            term = lax.dot_general(left, inside, (((1,), (1,)), ((), ())), preferred_element_type=jnp.float32)
            total = term if total is None else total + term
        outs.append(total)
    return outs


def send_kernel(temp, cell, slot, coef, solid, temp_at, outgoing):
    got = take(temp[...], cell[...])
    temp_at[...] = got
    groups, kinds, width = outgoing.shape
    filled = put([got, coef[...], solid[...]], slot[...], groups, width)
    for which in range(kinds):
        for group in range(groups):
            outgoing[group, which : which + 1, :] = filled[which][group : group + 1, :]


def local_call(kernel, outs, *args):
    whole = pl.BlockSpec(memory_space=VMEM)
    return pl.pallas_call(
        kernel,
        out_shape=tuple(jax.ShapeDtypeStruct(o, jnp.float32) for o in outs),
        in_specs=[whole] * len(args),
        out_specs=(whole,) * len(outs),
        name=kernel.__name__,
    )(*args)


def wall_kernel(
    sizes, outgoing, source, ambient, conduct, slot, cell, coef, temp_at, solid_out, flux_out,
    arrived, back, returned, residual, image, face_y, face_z, got_x, got_y, got_z, part, whole, held_x, held_g,
    own_sem, pair_send, pair_recv, back_send, back_recv, face_send, face_recv, x_send, x_recv, g_send, g_recv,
):
    count_x, count_y, count_z = sizes
    groups = count_y * count_z
    my_x, my_y, my_z = (lax.axis_index(axis) for axis in AXES)
    me = my_y * count_z + my_z
    mesh = pl.DeviceIdType.MESH
    size_x, size_y, size_z = source.shape

    def mate(step):
        other = lax.rem(me + step, groups)
        return (my_x, other // count_z, lax.rem(other, count_z))

    def row(step):
        return (lax.rem(my_x + step, count_x), my_y, my_z)

    def remote(src, dst, send, recv, device):
        return pltpu.make_async_remote_copy(
            src_ref=src, dst_ref=dst, send_sem=send, recv_sem=recv, device_id=device, device_id_type=mesh
        )

    barrier = pltpu.get_barrier_semaphore()
    for step in range(1, groups):
        pl.semaphore_signal(barrier, inc=1, device_id=mate(step), device_id_type=mesh)
    for step in range(1, count_x):
        pl.semaphore_signal(barrier, inc=1, device_id=row(step), device_id_type=mesh)
    pl.semaphore_wait(barrier, groups + count_x - 2)

    pairs = [
        remote(
            outgoing.at[lax.rem(me + step, groups)], arrived.at[step], pair_send.at[step], pair_recv.at[step], mate(step)
        )
        for step in range(1, groups)
    ]
    for copy in pairs:
        copy.start()
    own = pltpu.make_async_copy(outgoing.at[me], arrived.at[0], own_sem.at[0])
    own.start()

    y_next = (my_x, lax.rem(my_y + 1, count_y), my_z)
    y_last = (my_x, lax.rem(my_y + count_y - 1, count_y), my_z)
    z_next = (my_x, my_y, lax.rem(my_z + 1, count_z))
    z_last = (my_x, my_y, lax.rem(my_z + count_z - 1, count_z))

    def send_faces(which, field):
        value = field[...]
        face_y[which, 0] = value[:, 0, :]
        face_y[which, 1] = value[:, size_y - 1, :]
        turned = jnp.transpose(value.reshape(size_x * size_y, size_z))
        face_z[which, 0] = turned[0:8]
        face_z[which, 1] = turned[size_z - 8 : size_z]
        plan = (
            (field.at[size_x - 1], got_x.at[which, 0], row(1)),
            (field.at[0], got_x.at[which, 1], row(count_x - 1)),
            (face_y.at[which, 1], got_y.at[which, 0], y_next),
            (face_y.at[which, 0], got_y.at[which, 1], y_last),
            (face_z.at[which, 1], got_z.at[which, 0], z_next),
            (face_z.at[which, 0], got_z.at[which, 1], z_last),
        )
        copies = [
            remote(src, dst, face_send.at[which, at], face_recv.at[which, at], device)
            for at, (src, dst, device) in enumerate(plan)
        ]
        for copy in copies:
            copy.start()
        return copies

    def around(which, field, copies):
        for copy in copies:
            copy.wait()
        value = field[...]
        below_x = jnp.concatenate([got_x[which, 0][None], value[:-1]], axis=0)
        above_x = jnp.concatenate([value[1:], got_x[which, 1][None]], axis=0)
        at_y = lax.broadcasted_iota(jnp.int32, value.shape, 1)
        below_y = jnp.where(at_y == 0, got_y[which, 0][:, None, :], pltpu.roll(value, 1, 1))
        above_y = jnp.where(at_y == size_y - 1, got_y[which, 1][:, None, :], pltpu.roll(value, size_y - 1, 1))
        at_z = lax.broadcasted_iota(jnp.int32, value.shape, 2)

        def column(line):
            return jnp.transpose(jnp.broadcast_to(line, (size_z, size_x * size_y))).reshape(value.shape)

        below_z = jnp.where(at_z == 0, column(got_z[which, 0][7:8]), pltpu.roll(value, 1, 2))
        above_z = jnp.where(at_z == size_z - 1, column(got_z[which, 1][0:1]), pltpu.roll(value, size_z - 1, 2))
        return (above_x, below_x, above_y, below_y, above_z, below_z)

    conduct_copies = send_faces(0, conduct)
    conducts = around(0, conduct, conduct_copies)
    at_x, at_y, at_z = (lax.broadcasted_iota(jnp.int32, source.shape, dim) for dim in range(3))
    place_x, place_y, place_z = at_x + my_x * size_x, at_y + my_y * size_y, at_z + my_z * size_z
    inside = (
        place_x < count_x * size_x - 1, place_x > 0,
        place_y < count_y * size_y - 1, place_y > 0,
        place_z < count_z * size_z - 1, place_z > 0,
    )
    here = conduct[...]
    weights = [jnp.where(ok, 2.0 * here * other / (here + other), 0.0) for ok, other in zip(inside, conducts)]

    own.wait()
    for copy in pairs:
        copy.wait()
    landed = jnp.concatenate([arrived[step] for step in range(groups)], axis=1)
    solid_cell = (landed[2:3, :] + 0.5).astype(jnp.int32)
    gain, inflow = put([landed[1:2, :], landed[1:2, :] * landed[0:1, :]], solid_cell, size_x * size_y, size_z)
    residual[...] = source[...] + inflow.reshape(source.shape)
    diagonal = ambient[...] + gain.reshape(source.shape)

    def operate(which, field, copies):
        value = field[...]
        total = diagonal * value
        for weight, other in zip(weights, around(which, field, copies)):
            total = total + weight * (value - other)
        return total

    image[...] = operate(1, residual, send_faces(1, residual))
    twice = operate(2, image, send_faces(2, image))

    first, second = residual[...], image[...]
    products = [jnp.sum(jnp.sum(a * b, axis=0), axis=0, keepdims=True)
                for a, b in ((first, first), (first, second), (second, second), (second, twice))]
    part[...] = jnp.concatenate(products + products, axis=0)
    copies = [remote(part, held_x.at[step], x_send.at[step], x_recv.at[step], row(step)) for step in range(1, count_x)]
    for copy in copies:
        copy.start()
    total = part[...]
    for step, copy in enumerate(copies):
        copy.wait()
        total = total + held_x[step + 1]
    whole[...] = total
    copies = [remote(whole, held_g.at[step], g_send.at[step], g_recv.at[step], mate(step)) for step in range(1, groups)]
    for copy in copies:
        copy.start()
    for step, copy in enumerate(copies):
        copy.wait()
        total = total + held_g[step + 1]
    total = jnp.broadcast_to(jnp.sum(total, axis=1, keepdims=True), total.shape)
    norm, product, square, cross = (total[at : at + 1] for at in range(4))
    alpha = norm / product
    norm_next = norm - 2.0 * alpha * product + alpha * alpha * square
    product_next = product - 2.0 * alpha * square + alpha * alpha * cross
    ratio = norm_next / norm
    alpha_next = norm_next / (product_next - ratio * norm_next / alpha)
    on_first = alpha + alpha_next * (1.0 + ratio)
    on_second = alpha_next * alpha
    flat = (size_x * size_y, size_z)
    solid = on_first * first.reshape(flat) - on_second * second.reshape(flat)
    solid_out[...] = solid.reshape(source.shape)

    wall = take(solid, solid_cell)
    width = returned.shape[2]
    for step in range(groups):
        back[step] = wall[:, step * width : (step + 1) * width]
    copies = [
        remote(back.at[step], returned.at[me], back_send.at[step], back_recv.at[step], mate(groups - step))
        for step in range(1, groups)
    ]
    for copy in copies:
        copy.start()
    own = pltpu.make_async_copy(back.at[0], returned.at[me], own_sem.at[1])
    own.start()
    own.wait()
    for copy in copies:
        copy.wait()
    table = jnp.concatenate([returned[group] for group in range(groups)], axis=0)
    flux = coef[...] * (take(table, slot[...]) - temp_at[...])
    rows, lanes = flux_out.shape
    flux_out[...] = put([flux], cell[...], rows, lanes)[0]


def run_wall(fluid_flat, outgoing, source, *rest):
    sizes = tuple(lax.axis_size(axis) for axis in AXES)
    groups, kinds, width = outgoing.shape
    size_x, size_y, size_z = source.shape
    count_x = sizes[0]
    block = pl.BlockSpec(memory_space=VMEM)
    dma = pltpu.SemaphoreType.DMA

    def f32(*shape):
        return VMEM(shape, jnp.float32)

    return pl.pallas_call(
        functools.partial(wall_kernel, sizes),
        out_shape=(jax.ShapeDtypeStruct(source.shape, jnp.float32), jax.ShapeDtypeStruct(fluid_flat, jnp.float32)),
        in_specs=[block] * (2 + len(rest)),
        out_specs=(block, block),
        scratch_shapes=[
            f32(groups, kinds, width), f32(groups, 1, width), f32(groups, 1, width),
            f32(*source.shape), f32(*source.shape),
            f32(3, 2, size_x, size_z), f32(3, 2, 8, size_x * size_y),
            f32(3, 2, size_y, size_z), f32(3, 2, size_x, size_z), f32(3, 2, 8, size_x * size_y),
            f32(8, size_z), f32(8, size_z), f32(count_x, 8, size_z), f32(groups, 8, size_z),
            dma((2,)), dma((groups,)), dma((groups,)), dma((groups,)), dma((groups,)),
            dma((3, 6)), dma((3, 6)), dma((count_x,)), dma((count_x,)), dma((groups,)), dma((groups,)),
        ],
        compiler_params=pltpu.CompilerParams(collective_id=0, has_side_effects=True),
        name="wall",
    )(outgoing, source, *rest)


def per_device(
    density_start,
    velocity_start,
    temp_start,
    block_level,
    solid_source,
    ambient,
    conduct,
    pair_cell,
    pair_dest,
    pair_solid,
    pair_coef,
):
    size_x, size_y, size_z = density_start.shape
    blocks_x, blocks_y, blocks_z = block_level.shape
    fine = jnp.broadcast_to(
        (block_level == 1)[:, None, :, None, :, None], (blocks_x, BLK, blocks_y, BLK, blocks_z, BLK)
    ).reshape(size_x, size_y, size_z)
    fields = jnp.stack(
        [density_start, velocity_start[0], velocity_start[1], velocity_start[2], temp_start, fine.astype(jnp.float32)]
    )
    count = lax.axis_size("gx")
    fields = jnp.concatenate(
        [
            lax.ppermute(fields[:, -HALO:], "gx", [(i, (i + 1) % count) for i in range(count)]),
            fields,
            lax.ppermute(fields[:, :HALO], "gx", [((i + 1) % count, i) for i in range(count)]),
        ],
        axis=1,
    )
    fields = ring_halo(fields, "gy", 2, size_y + 8)
    fields = ring_halo(fields, "gz", 3, size_z + 128)
    fluid_temp, fluid_vel = run_fluid(fields, (size_x, size_y, size_z))

    groups = lax.axis_size(("gy", "gz"))
    pair_count = pair_cell.shape[0]
    capacity = 2 * pair_count // groups
    dest = pair_dest[:, 0]
    onehot = (dest[:, None] == jnp.arange(groups, dtype=jnp.int32)[None, :]).astype(jnp.int32)
    rank = jnp.sum((jnp.cumsum(onehot, axis=0) - onehot) * onehot, axis=1)
    width = -(-capacity // size_z) * size_z
    slot = (dest * width + rank)[None, :]
    cell = pair_cell[None, :]
    coef = pair_coef[None, :]
    solid = pair_solid.astype(jnp.float32)[None, :]
    flat = (size_x * size_y, size_z)
    temp_at, outgoing = local_call(
        send_kernel, ((1, pair_count), (groups, 3, width)), fluid_temp.reshape(flat), cell, slot, coef, solid
    )
    solid_temp, wall_flux = run_wall(
        flat, outgoing, solid_source, ambient, conduct, slot, cell, coef, temp_at
    )
    return (fluid_temp, fluid_vel, solid_temp, wall_flux.reshape(size_x, size_y, size_z))


def solution(mesh):
    return jax.shard_map(
        per_device,
        mesh=mesh,
        in_specs=(
            P("gx", "gy", "gz"),
            P(None, "gx", "gy", "gz"),
            P("gx", "gy", "gz"),
            P("gx", "gy", "gz"),
            P("gx", "gy", "gz"),
            P("gx", "gy", "gz"),
            P("gx", "gy", "gz"),
            P(("gx", "gy", "gz")),
            P(("gx", "gy", "gz"), None),
            P(("gx", "gy", "gz")),
            P(("gx", "gy", "gz")),
        ),
        out_specs=(
            P("gx", "gy", "gz"),
            P(None, "gx", "gy", "gz"),
            P("gx", "gy", "gz"),
            P("gx", "gy", "gz"),
        ),
        check_vma=False,
    )
```

```python
import functools

import jax
import jax.numpy as jnp
from jax import lax
from jax.experimental import pallas as pl
from jax.experimental.pallas import tpu as pltpu
from jax.sharding import PartitionSpec as P

BLK = 16
ITERS = 2


velocity_set = (
    (0, 0, 0),
    (1, 0, 0),
    (-1, 0, 0),
    (0, 1, 0),
    (0, -1, 0),
    (0, 0, 1),
    (0, 0, -1),
    (1, 1, 0),
    (-1, -1, 0),
    (1, -1, 0),
    (-1, 1, 0),
    (1, 0, 1),
    (-1, 0, -1),
    (1, 0, -1),
    (-1, 0, 1),
    (0, 1, 1),
    (0, -1, -1),
    (0, 1, -1),
    (0, -1, 1),
)
weight_flow = (1.0 / 3.0,) + (1.0 / 18.0,) * 6 + (1.0 / 36.0,) * 12
weight_heat = (0.25,) + (0.125,) * 6
stacked_set = velocity_set + velocity_set[:7]


AXES = ("gx", "gy", "gz")
HALO = 2
VMEM = pltpu.VMEM


def halo_kernel(sizes, cells, fields, got_x, pack_y, got_y, pack_z, got_z, send_sem, recv_sem):
    kinds, size_x, size_y, size_z = cells.shape
    planes = fields.shape[1]
    spots = [lax.axis_index(axis) for axis in AXES]
    mesh = pl.DeviceIdType.MESH

    def beside(axis, step):
        moved = list(spots)
        moved[axis] = lax.rem(spots[axis] + (sizes[axis] + step), sizes[axis])
        return tuple(moved)

    barrier = pltpu.get_barrier_semaphore()
    for axis in range(3):
        for step in (1, -1):
            pl.semaphore_signal(barrier, inc=1, device_id=beside(axis, step), device_id_type=mesh)
    pl.semaphore_wait(barrier, 6)

    def both(axis, up, down, got):
        copies = [
            pltpu.make_async_remote_copy(
                src_ref=src, dst_ref=got.at[side], send_sem=send_sem.at[axis, side], recv_sem=recv_sem.at[axis, side],
                device_id=beside(axis, step), device_id_type=mesh,
            )
            for side, (src, step) in enumerate(((up, 1), (down, -1)))
        ]
        if sizes[axis] == 2 and up is down:
            copies = copies[:1]
        for copy in copies:
            copy.start()
        return copies

    def finish(copies):
        for copy in copies:
            copy.wait()

    copies = both(0, cells.at[:, pl.ds(size_x - HALO, HALO)], cells.at[:, pl.ds(0, HALO)], got_x)
    for kind in range(kinds):
        fields[kind, HALO : HALO + size_x, :size_y, :size_z] = cells[kind]
    finish(copies)
    for kind in range(kinds):
        fields[kind, :HALO, :size_y, :size_z] = got_x[0, kind]
        fields[kind, HALO + size_x :, :size_y, :size_z] = got_x[1, kind]

    row = lax.broadcasted_iota(jnp.int32, (8, size_z), 0)

    def ends(kind, plane):
        return jnp.where(row < 4, fields[kind, plane, 0:8, :size_z], fields[kind, plane, size_y - 8 : size_y, :size_z])

    for kind in range(kinds):

        def pack(pair, carry):
            even = pltpu.roll(ends(kind, 2 * pair), 2, 0)
            odd = pltpu.roll(ends(kind, 2 * pair + 1), 6, 0)
            pack_y[kind, pair] = jnp.where(row < 4, even, odd)
            return carry

        lax.fori_loop(0, planes // 2, pack, 0, unroll=True)
    copies = both(1, pack_y, pack_y, got_y)
    finish(copies)
    next_y = 1 if len(copies) == 2 else 0
    for kind in range(kinds):

        def unpack(pair, carry):
            mixed = jnp.where(row % 4 < 2, got_y[0, kind, pair], got_y[next_y, kind, pair])
            fields[kind, 2 * pair, size_y:, :size_z] = pltpu.roll(mixed, 6, 0)
            fields[kind, 2 * pair + 1, size_y:, :size_z] = pltpu.roll(mixed, 2, 0)
            return carry

        lax.fori_loop(0, planes // 2, unpack, 0, unroll=True)

    per = size_z // 4
    lane = lax.broadcasted_iota(jnp.int32, (size_y + 8, size_z), 1)
    for group in range(pack_z.shape[0]):
        total = jnp.zeros((size_y + 8, size_z), jnp.float32)
        for spot in range(min(per, kinds * planes - group * per)):
            kind, plane = divmod(group * per + spot, planes)
            moved = pltpu.roll(fields[kind, plane, :, :size_z], (4 * spot + 2) % size_z, 1)
            total = jnp.where(lane // 4 == spot, moved, total)
        pack_z[group] = total
    copies = both(2, pack_z, pack_z, got_z)
    finish(copies)
    next_z = 1 if len(copies) == 2 else 0
    for group in range(pack_z.shape[0]):
        mixed = jnp.where(lane % 4 < 2, got_z[0, group], got_z[next_z, group])
        for spot in range(min(per, kinds * planes - group * per)):
            kind, plane = divmod(group * per + spot, planes)
            fields[kind, plane, :, size_z:] = pltpu.roll(mixed, (size_z - 4 * spot - 2) % size_z, 1)


def run_halo(cells):
    sizes = tuple(lax.axis_size(axis) for axis in AXES)
    kinds, size_x, size_y, size_z = cells.shape
    planes = size_x + 2 * HALO
    groups = -(-kinds * planes // (size_z // 4))
    block = pl.BlockSpec(memory_space=VMEM)
    dma = pltpu.SemaphoreType.DMA

    def f32(*shape):
        return VMEM(shape, jnp.float32)

    return pl.pallas_call(
        functools.partial(halo_kernel, sizes),
        out_shape=jax.ShapeDtypeStruct((kinds, planes, size_y + 8, 2 * size_z), jnp.float32),
        in_specs=[block],
        out_specs=block,
        scratch_shapes=[
            f32(2, kinds, HALO, size_y, size_z),
            f32(kinds, planes // 2, 8, size_z), f32(2, kinds, planes // 2, 8, size_z),
            f32(groups, size_y + 8, size_z), f32(2, groups, size_y + 8, size_z),
            dma((3, 2)), dma((3, 2)),
        ],
        compiler_params=pltpu.CompilerParams(collective_id=1, has_side_effects=True),
        name="halo",
    )(cells)


def along_of(which, speed):
    along = None
    for dimen in range(3):
        sign = velocity_set[which][dimen]
        if sign == 1:
            along = speed[dimen] if along is None else along + speed[dimen]
        elif sign == -1:
            along = -speed[dimen] if along is None else along - speed[dimen]
    return along


def equilibrium(density, speed):
    square = 1.0 - 1.5 * (speed[0] * speed[0] + speed[1] * speed[1] + speed[2] * speed[2])
    weighted = {w: w * density for w in set(weight_flow)}
    rows_out = [weighted[weight_flow[0]] * square]
    for which in range(1, 19, 2):
        along = along_of(which, speed)
        rho = weighted[weight_flow[which]]
        even = rho * (square + 4.5 * along * along)
        odd = rho * (3.0 * along)
        rows_out += [even + odd, even - odd]
    return rows_out


def heat_equilibrium(temper, speed):
    rows_out = [weight_heat[0] * temper]
    for which in range(1, 7, 2):
        even = weight_heat[which] * temper
        odd = even * (4.0 * along_of(which, speed))
        rows_out += [even + odd, even - odd]
    return rows_out


def flow_moments(flow):
    density = flow[0]
    for which in range(1, 19):
        density = density + flow[which]
    inverse = 1.0 / density
    speed = []
    for dimen in range(3):
        total = None
        for which in range(19):
            sign = velocity_set[which][dimen]
            if sign == 1:
                total = flow[which] if total is None else total + flow[which]
            elif sign == -1:
                total = total - flow[which]
        speed.append(total * inverse)
    return density, speed


def collide(flow, heat, rate_flow, rate_heat):
    density, speed = flow_moments(flow)
    temper = functools.reduce(lambda a, b: a + b, heat)
    flow = [f - rate_flow * (f - e) for f, e in zip(flow, equilibrium(density, speed))]
    heat = [g - rate_heat * (g - e) for g, e in zip(heat, heat_equilibrium(temper, speed))]
    return flow, heat


def stream_plane(store, plane, values):
    height, width = values[0].shape
    for which, value in enumerate(values):
        off_x, off_y, off_z = stacked_set[which]
        if off_y:
            value = pltpu.roll(value, off_y % height, 0)
        if off_z:
            value = pltpu.roll(value, off_z % width, 1)
        store[which, plane + off_x + 1] = value


def fluid_kernel(fields, temp_out, vel_out, first, second):
    planes = fields.shape[1]
    size_x, size_y, size_z = temp_out.shape

    def one(plane, carry):
        density = fields[0, plane]
        speed = [fields[1, plane], fields[2, plane], fields[3, plane]]
        fine = fields[5, plane] == 1.0
        flow, heat = collide(
            equilibrium(density, speed),
            heat_equilibrium(fields[4, plane], speed),
            jnp.where(fine, 1.0 / 1.3, 1.0 / 0.9),
            jnp.where(fine, 1.0 / 1.1, 1.0 / 0.8),
        )
        stream_plane(first, plane, flow + heat)
        return carry

    def two(plane, carry):
        fine = fields[5, plane] == 1.0
        values = [first[which, plane + 1] for which in range(26)]
        flow, heat = collide(
            values[:19], values[19:], jnp.where(fine, 1.0 / 1.3, 0.0), jnp.where(fine, 1.0 / 1.1, 0.0)
        )
        stream_plane(second, plane, flow + heat)
        return carry

    def three(row, carry):
        plane = row + HALO + 1
        values = [second[which, plane, :size_y, :size_z] for which in range(26)]
        density, speed = flow_moments(values[:19])
        temp_out[row] = functools.reduce(lambda a, b: a + b, values[19:])
        for dimen in range(3):
            vel_out[dimen, row] = speed[dimen]
        return carry

    lax.fori_loop(0, planes, one, 0)
    lax.fori_loop(1, planes - 1, two, 0)
    lax.fori_loop(0, size_x, three, 0)


def run_fluid(fields, shape):
    planes, height, width = fields.shape[1:]
    whole = pl.BlockSpec(memory_space=VMEM)
    return pl.pallas_call(
        fluid_kernel,
        out_shape=(jax.ShapeDtypeStruct(shape, jnp.float32), jax.ShapeDtypeStruct((3,) + shape, jnp.float32)),
        in_specs=[whole],
        out_specs=(whole, whole),
        scratch_shapes=[VMEM((26, planes + 2, height, width), jnp.float32)] * 2,
        compiler_params=pltpu.CompilerParams(vmem_limit_bytes=52 * 1024 * 1024),
        name="fluid",
    )(fields)


def thirds(value):
    high = value.astype(jnp.bfloat16)
    rest = value - high.astype(jnp.float32)
    middle = rest.astype(jnp.bfloat16)
    low = (rest - middle.astype(jnp.float32)).astype(jnp.bfloat16)
    return [high, middle, low]


def one_hot(index, count):
    rows = lax.broadcasted_iota(jnp.int32, (count, index.shape[1]), 0)
    return rows == index


def take(table, index):
    rows, lanes = table.shape
    pick = one_hot(index // lanes, rows).astype(jnp.float32).astype(jnp.bfloat16)
    inside = one_hot(index % lanes, lanes)
    got = None
    for part in thirds(table):
        term = lax.dot_general(part, pick, (((0,), (0,)), ((), ())), preferred_element_type=jnp.float32)
        got = term if got is None else got + term
    return jnp.sum(jnp.where(inside, got, 0.0), axis=0, keepdims=True)


def put(values, index, rows, lanes):
    hot = one_hot(index // lanes, rows).astype(jnp.float32)
    inside = one_hot(index % lanes, lanes).astype(jnp.float32).astype(jnp.bfloat16)
    outs = []
    for value in values:
        total = None
        for part in thirds(value):
            left = (hot * part.astype(jnp.float32)).astype(jnp.bfloat16)
            term = lax.dot_general(left, inside, (((1,), (1,)), ((), ())), preferred_element_type=jnp.float32)
            total = term if total is None else total + term
        outs.append(total)
    return outs


def send_kernel(temp, cell, slot, coef, solid, temp_at, outgoing):
    got = take(temp[...], cell[...])
    temp_at[...] = got
    groups, kinds, width = outgoing.shape
    filled = put([got, coef[...], solid[...]], slot[...], groups, width)
    for which in range(kinds):
        for group in range(groups):
            outgoing[group, which : which + 1, :] = filled[which][group : group + 1, :]


def local_call(kernel, outs, *args):
    whole = pl.BlockSpec(memory_space=VMEM)
    return pl.pallas_call(
        kernel,
        out_shape=tuple(jax.ShapeDtypeStruct(o, jnp.float32) for o in outs),
        in_specs=[whole] * len(args),
        out_specs=(whole,) * len(outs),
        name=kernel.__name__,
    )(*args)


def wall_kernel(
    sizes, outgoing, source, ambient, conduct, slot, cell, coef, temp_at, solid_out, flux_out,
    arrived, back, returned, residual, image, face_y, face_z, got_x, got_y, got_z, part, whole, held_x, held_g,
    own_sem, pair_send, pair_recv, back_send, back_recv, face_send, face_recv, x_send, x_recv, g_send, g_recv,
):
    count_x, count_y, count_z = sizes
    groups = count_y * count_z
    my_x, my_y, my_z = (lax.axis_index(axis) for axis in AXES)
    me = my_y * count_z + my_z
    mesh = pl.DeviceIdType.MESH
    size_x, size_y, size_z = source.shape

    def mate(step):
        other = lax.rem(me + step, groups)
        return (my_x, other // count_z, lax.rem(other, count_z))

    def row(step):
        return (lax.rem(my_x + step, count_x), my_y, my_z)

    def remote(src, dst, send, recv, device):
        return pltpu.make_async_remote_copy(
            src_ref=src, dst_ref=dst, send_sem=send, recv_sem=recv, device_id=device, device_id_type=mesh
        )

    barrier = pltpu.get_barrier_semaphore()
    for step in range(1, groups):
        pl.semaphore_signal(barrier, inc=1, device_id=mate(step), device_id_type=mesh)
    for step in range(1, count_x):
        pl.semaphore_signal(barrier, inc=1, device_id=row(step), device_id_type=mesh)
    pl.semaphore_wait(barrier, groups + count_x - 2)

    pairs = [
        remote(
            outgoing.at[lax.rem(me + step, groups)], arrived.at[step], pair_send.at[step], pair_recv.at[step], mate(step)
        )
        for step in range(1, groups)
    ]
    for copy in pairs:
        copy.start()
    own = pltpu.make_async_copy(outgoing.at[me], arrived.at[0], own_sem.at[0])
    own.start()

    y_next = (my_x, lax.rem(my_y + 1, count_y), my_z)
    y_last = (my_x, lax.rem(my_y + count_y - 1, count_y), my_z)
    z_next = (my_x, my_y, lax.rem(my_z + 1, count_z))
    z_last = (my_x, my_y, lax.rem(my_z + count_z - 1, count_z))

    def send_faces(which, field):
        value = field[...]
        face_y[which, 0] = value[:, 0, :]
        face_y[which, 1] = value[:, size_y - 1, :]
        turned = jnp.transpose(value.reshape(size_x * size_y, size_z))
        face_z[which, 0] = turned[0:8]
        face_z[which, 1] = turned[size_z - 8 : size_z]
        plan = (
            (field.at[size_x - 1], got_x.at[which, 0], row(1)),
            (field.at[0], got_x.at[which, 1], row(count_x - 1)),
            (face_y.at[which, 1], got_y.at[which, 0], y_next),
            (face_y.at[which, 0], got_y.at[which, 1], y_last),
            (face_z.at[which, 1], got_z.at[which, 0], z_next),
            (face_z.at[which, 0], got_z.at[which, 1], z_last),
        )
        copies = [
            remote(src, dst, face_send.at[which, at], face_recv.at[which, at], device)
            for at, (src, dst, device) in enumerate(plan)
        ]
        for copy in copies:
            copy.start()
        return copies

    def around(which, field, copies):
        for copy in copies:
            copy.wait()
        value = field[...]
        below_x = jnp.concatenate([got_x[which, 0][None], value[:-1]], axis=0)
        above_x = jnp.concatenate([value[1:], got_x[which, 1][None]], axis=0)
        at_y = lax.broadcasted_iota(jnp.int32, value.shape, 1)
        below_y = jnp.where(at_y == 0, got_y[which, 0][:, None, :], pltpu.roll(value, 1, 1))
        above_y = jnp.where(at_y == size_y - 1, got_y[which, 1][:, None, :], pltpu.roll(value, size_y - 1, 1))
        at_z = lax.broadcasted_iota(jnp.int32, value.shape, 2)

        def column(line):
            return jnp.transpose(jnp.broadcast_to(line, (size_z, size_x * size_y))).reshape(value.shape)

        below_z = jnp.where(at_z == 0, column(got_z[which, 0][7:8]), pltpu.roll(value, 1, 2))
        above_z = jnp.where(at_z == size_z - 1, column(got_z[which, 1][0:1]), pltpu.roll(value, size_z - 1, 2))
        return (above_x, below_x, above_y, below_y, above_z, below_z)

    conduct_copies = send_faces(0, conduct)
    conducts = around(0, conduct, conduct_copies)
    at_x, at_y, at_z = (lax.broadcasted_iota(jnp.int32, source.shape, dim) for dim in range(3))
    place_x, place_y, place_z = at_x + my_x * size_x, at_y + my_y * size_y, at_z + my_z * size_z
    inside = (
        place_x < count_x * size_x - 1, place_x > 0,
        place_y < count_y * size_y - 1, place_y > 0,
        place_z < count_z * size_z - 1, place_z > 0,
    )
    here = conduct[...]
    weights = [jnp.where(ok, 2.0 * here * other / (here + other), 0.0) for ok, other in zip(inside, conducts)]

    own.wait()
    for copy in pairs:
        copy.wait()
    landed = jnp.concatenate([arrived[step] for step in range(groups)], axis=1)
    solid_cell = (landed[2:3, :] + 0.5).astype(jnp.int32)
    gain, inflow = put([landed[1:2, :], landed[1:2, :] * landed[0:1, :]], solid_cell, size_x * size_y, size_z)
    residual[...] = source[...] + inflow.reshape(source.shape)
    diagonal = ambient[...] + gain.reshape(source.shape)

    def operate(which, field, copies):
        value = field[...]
        total = diagonal * value
        for weight, other in zip(weights, around(which, field, copies)):
            total = total + weight * (value - other)
        return total

    image[...] = operate(1, residual, send_faces(1, residual))
    twice = operate(2, image, send_faces(2, image))

    first, second = residual[...], image[...]
    products = [jnp.sum(jnp.sum(a * b, axis=0), axis=0, keepdims=True)
                for a, b in ((first, first), (first, second), (second, second), (second, twice))]
    part[...] = jnp.concatenate(products + products, axis=0)
    copies = [remote(part, held_x.at[step], x_send.at[step], x_recv.at[step], row(step)) for step in range(1, count_x)]
    for copy in copies:
        copy.start()
    total = part[...]
    for step, copy in enumerate(copies):
        copy.wait()
        total = total + held_x[step + 1]
    whole[...] = total
    copies = [remote(whole, held_g.at[step], g_send.at[step], g_recv.at[step], mate(step)) for step in range(1, groups)]
    for copy in copies:
        copy.start()
    for step, copy in enumerate(copies):
        copy.wait()
        total = total + held_g[step + 1]
    total = jnp.broadcast_to(jnp.sum(total, axis=1, keepdims=True), total.shape)
    norm, product, square, cross = (total[at : at + 1] for at in range(4))
    alpha = norm / product
    norm_next = norm - 2.0 * alpha * product + alpha * alpha * square
    product_next = product - 2.0 * alpha * square + alpha * alpha * cross
    ratio = norm_next / norm
    alpha_next = norm_next / (product_next - ratio * norm_next / alpha)
    on_first = alpha + alpha_next * (1.0 + ratio)
    on_second = alpha_next * alpha
    flat = (size_x * size_y, size_z)
    solid = on_first * first.reshape(flat) - on_second * second.reshape(flat)
    solid_out[...] = solid.reshape(source.shape)

    wall = take(solid, solid_cell)
    width = returned.shape[2]
    for step in range(groups):
        back[step] = wall[:, step * width : (step + 1) * width]
    copies = [
        remote(back.at[step], returned.at[me], back_send.at[step], back_recv.at[step], mate(groups - step))
        for step in range(1, groups)
    ]
    for copy in copies:
        copy.start()
    own = pltpu.make_async_copy(back.at[0], returned.at[me], own_sem.at[1])
    own.start()
    own.wait()
    for copy in copies:
        copy.wait()
    table = jnp.concatenate([returned[group] for group in range(groups)], axis=0)
    flux = coef[...] * (take(table, slot[...]) - temp_at[...])
    rows, lanes = flux_out.shape
    flux_out[...] = put([flux], cell[...], rows, lanes)[0]


def run_wall(fluid_flat, outgoing, source, *rest):
    sizes = tuple(lax.axis_size(axis) for axis in AXES)
    groups, kinds, width = outgoing.shape
    size_x, size_y, size_z = source.shape
    count_x = sizes[0]
    block = pl.BlockSpec(memory_space=VMEM)
    dma = pltpu.SemaphoreType.DMA

    def f32(*shape):
        return VMEM(shape, jnp.float32)

    return pl.pallas_call(
        functools.partial(wall_kernel, sizes),
        out_shape=(jax.ShapeDtypeStruct(source.shape, jnp.float32), jax.ShapeDtypeStruct(fluid_flat, jnp.float32)),
        in_specs=[block] * (2 + len(rest)),
        out_specs=(block, block),
        scratch_shapes=[
            f32(groups, kinds, width), f32(groups, 1, width), f32(groups, 1, width),
            f32(*source.shape), f32(*source.shape),
            f32(3, 2, size_x, size_z), f32(3, 2, 8, size_x * size_y),
            f32(3, 2, size_y, size_z), f32(3, 2, size_x, size_z), f32(3, 2, 8, size_x * size_y),
            f32(8, size_z), f32(8, size_z), f32(count_x, 8, size_z), f32(groups, 8, size_z),
            dma((2,)), dma((groups,)), dma((groups,)), dma((groups,)), dma((groups,)),
            dma((3, 6)), dma((3, 6)), dma((count_x,)), dma((count_x,)), dma((groups,)), dma((groups,)),
        ],
        compiler_params=pltpu.CompilerParams(collective_id=0, has_side_effects=True),
        name="wall",
    )(outgoing, source, *rest)


def per_device(
    density_start,
    velocity_start,
    temp_start,
    block_level,
    solid_source,
    ambient,
    conduct,
    pair_cell,
    pair_dest,
    pair_solid,
    pair_coef,
):
    size_x, size_y, size_z = density_start.shape
    blocks_x, blocks_y, blocks_z = block_level.shape
    fine = jnp.broadcast_to(
        (block_level == 1)[:, None, :, None, :, None], (blocks_x, BLK, blocks_y, BLK, blocks_z, BLK)
    ).reshape(size_x, size_y, size_z)
    fields = jnp.stack(
        [density_start, velocity_start[0], velocity_start[1], velocity_start[2], temp_start, fine.astype(jnp.float32)]
    )
    fields = run_halo(fields)
    fluid_temp, fluid_vel = run_fluid(fields, (size_x, size_y, size_z))

    groups = lax.axis_size(("gy", "gz"))
    pair_count = pair_cell.shape[0]
    capacity = 2 * pair_count // groups
    dest = pair_dest[:, 0]
    onehot = (dest[:, None] == jnp.arange(groups, dtype=jnp.int32)[None, :]).astype(jnp.int32)
    rank = jnp.sum((jnp.cumsum(onehot, axis=0) - onehot) * onehot, axis=1)
    width = -(-capacity // size_z) * size_z
    slot = (dest * width + rank)[None, :]
    cell = pair_cell[None, :]
    coef = pair_coef[None, :]
    solid = pair_solid.astype(jnp.float32)[None, :]
    flat = (size_x * size_y, size_z)
    temp_at, outgoing = local_call(
        send_kernel, ((1, pair_count), (groups, 3, width)), fluid_temp.reshape(flat), cell, slot, coef, solid
    )
    solid_temp, wall_flux = run_wall(
        flat, outgoing, solid_source, ambient, conduct, slot, cell, coef, temp_at
    )
    return (fluid_temp, fluid_vel, solid_temp, wall_flux.reshape(size_x, size_y, size_z))


def solution(mesh):
    return jax.shard_map(
        per_device,
        mesh=mesh,
        in_specs=(
            P("gx", "gy", "gz"),
            P(None, "gx", "gy", "gz"),
            P("gx", "gy", "gz"),
            P("gx", "gy", "gz"),
            P("gx", "gy", "gz"),
            P("gx", "gy", "gz"),
            P("gx", "gy", "gz"),
            P(("gx", "gy", "gz")),
            P(("gx", "gy", "gz"), None),
            P(("gx", "gy", "gz")),
            P(("gx", "gy", "gz")),
        ),
        out_specs=(
            P("gx", "gy", "gz"),
            P(None, "gx", "gy", "gz"),
            P("gx", "gy", "gz"),
            P("gx", "gy", "gz"),
        ),
        check_vma=False,
    )
```

```python
import functools

import jax
import jax.numpy as jnp
from jax import lax
from jax.experimental import pallas as pl
from jax.experimental.pallas import tpu as pltpu
from jax.sharding import PartitionSpec as P

BLK = 16
ITERS = 2


velocity_set = (
    (0, 0, 0),
    (1, 0, 0),
    (-1, 0, 0),
    (0, 1, 0),
    (0, -1, 0),
    (0, 0, 1),
    (0, 0, -1),
    (1, 1, 0),
    (-1, -1, 0),
    (1, -1, 0),
    (-1, 1, 0),
    (1, 0, 1),
    (-1, 0, -1),
    (1, 0, -1),
    (-1, 0, 1),
    (0, 1, 1),
    (0, -1, -1),
    (0, 1, -1),
    (0, -1, 1),
)
weight_flow = (1.0 / 3.0,) + (1.0 / 18.0,) * 6 + (1.0 / 36.0,) * 12
weight_heat = (0.25,) + (0.125,) * 6
stacked_set = velocity_set + velocity_set[:7]


AXES = ("gx", "gy", "gz")
HALO = 2
VMEM = pltpu.VMEM


def halo_kernel(
    sizes, density, velocity, temper, fine, fields,
    got_x, pack_y, got_y, pack_c, got_c, pack_z, got_z, send_sem, recv_sem,
):
    size_x, size_y, size_z = density.shape
    kinds, planes = fields.shape[:2]
    spots = [lax.axis_index(axis) for axis in AXES]
    mesh = pl.DeviceIdType.MESH

    def beside(axis, step):
        moved = list(spots)
        moved[axis] = lax.rem(spots[axis] + (sizes[axis] + step), sizes[axis])
        return tuple(moved)

    barrier = pltpu.get_barrier_semaphore()
    for axis in range(3):
        for step in (1, -1):
            pl.semaphore_signal(barrier, inc=1, device_id=beside(axis, step), device_id_type=mesh)
    pl.semaphore_wait(barrier, 6)

    def both(number, axis, up, down, got):
        copies = [
            pltpu.make_async_remote_copy(
                src_ref=src, dst_ref=dst, send_sem=send_sem.at[number, side], recv_sem=recv_sem.at[number, side],
                device_id=beside(axis, step), device_id_type=mesh,
            )
            for side, (src, dst, step) in enumerate(((up, got[0], 1), (down, got[1], -1)))
            if side == 0 or sizes[axis] > 2 or up is not down
        ]
        for copy in copies:
            copy.start()
        return copies

    def finish(copies):
        for copy in copies:
            copy.wait()

    low, high = pl.ds(0, HALO), pl.ds(size_x - HALO, HALO)
    copies_x = []
    for number, (field, kind) in enumerate(((density, 0), (temper, 4), (fine, 5))):
        copies_x += both(number, 0, field.at[high], field.at[low], [got_x.at[side, kind] for side in range(2)])
    copies_x += both(
        3, 0, velocity.at[:, high], velocity.at[:, low], [got_x.at[side, pl.ds(1, 3)] for side in range(2)]
    )
    for kind, field in ((0, density), (4, temper), (5, fine)):
        fields[kind, HALO : HALO + size_x, :size_y, :size_z] = field[...]
    for kind in range(3):
        fields[kind + 1, HALO : HALO + size_x, :size_y, :size_z] = velocity[kind]

    row = lax.broadcasted_iota(jnp.int32, (8, size_z), 0)

    def packed(kind, plane):
        ends = [
            jnp.where(row < 4, fields[kind, at, 0:8, :size_z], fields[kind, at, size_y - 8 : size_y, :size_z])
            for at in (plane, plane + 1)
        ]
        return jnp.where(row < 4, pltpu.roll(ends[0], 2, 0), pltpu.roll(ends[1], 6, 0))

    def unpacked(kind, plane, below, above):
        mixed = jnp.where(row % 4 < 2, below, above)
        fields[kind, plane, size_y:, :size_z] = pltpu.roll(mixed, 6, 0)
        fields[kind, plane + 1, size_y:, :size_z] = pltpu.roll(mixed, 2, 0)

    for kind in range(kinds):
        for pair in range(size_x // 2):
            pack_y[kind, pair] = packed(kind, HALO + 2 * pair)
    copies_y = both(4, 1, pack_y, pack_y, [got_y.at[side] for side in range(2)])
    finish(copies_x)
    for kind in range(kinds):
        fields[kind, :HALO, :size_y, :size_z] = got_x[0, kind]
        fields[kind, HALO + size_x :, :size_y, :size_z] = got_x[1, kind]
    corners = (0, HALO + size_x)
    for kind in range(kinds):
        for corner, plane in enumerate(corners):
            pack_c[kind, corner] = packed(kind, plane)
    copies_c = both(5, 1, pack_c, pack_c, [got_c.at[side] for side in range(2)])
    next_y = len(copies_y) - 1
    finish(copies_y)
    for kind in range(kinds):
        for pair in range(size_x // 2):
            unpacked(kind, HALO + 2 * pair, got_y[0, kind, pair], got_y[next_y, kind, pair])
    finish(copies_c)
    for kind in range(kinds):
        for corner, plane in enumerate(corners):
            unpacked(kind, plane, got_c[0, kind, corner], got_c[next_y, kind, corner])

    per = size_z // 4
    lane = lax.broadcasted_iota(jnp.int32, (size_y + 8, size_z), 1)
    for group in range(pack_z.shape[0]):
        total = jnp.zeros((size_y + 8, size_z), jnp.float32)
        for spot in range(min(per, kinds * planes - group * per)):
            kind, plane = divmod(group * per + spot, planes)
            moved = pltpu.roll(fields[kind, plane, :, :size_z], (4 * spot + 2) % size_z, 1)
            total = jnp.where(lane // 4 == spot, moved, total)
        pack_z[group] = total
    copies = both(6, 2, pack_z, pack_z, [got_z.at[side] for side in range(2)])
    finish(copies)
    next_z = len(copies) - 1
    for group in range(pack_z.shape[0]):
        mixed = jnp.where(lane % 4 < 2, got_z[0, group], got_z[next_z, group])
        for spot in range(min(per, kinds * planes - group * per)):
            kind, plane = divmod(group * per + spot, planes)
            fields[kind, plane, :, size_z:] = pltpu.roll(mixed, (size_z - 4 * spot - 2) % size_z, 1)


def run_halo(density, velocity, temper, fine):
    sizes = tuple(lax.axis_size(axis) for axis in AXES)
    size_x, size_y, size_z = density.shape
    kinds = 6
    planes = size_x + 2 * HALO
    groups = -(-kinds * planes // (size_z // 4))
    block = pl.BlockSpec(memory_space=VMEM)
    dma = pltpu.SemaphoreType.DMA

    def f32(*shape):
        return VMEM(shape, jnp.float32)

    return pl.pallas_call(
        functools.partial(halo_kernel, sizes),
        out_shape=jax.ShapeDtypeStruct((kinds, planes, size_y + 8, 2 * size_z), jnp.float32),
        in_specs=[block] * 4,
        out_specs=block,
        scratch_shapes=[
            f32(2, kinds, HALO, size_y, size_z),
            f32(kinds, size_x // 2, 8, size_z), f32(2, kinds, size_x // 2, 8, size_z),
            f32(kinds, 2, 8, size_z), f32(2, kinds, 2, 8, size_z),
            f32(groups, size_y + 8, size_z), f32(2, groups, size_y + 8, size_z),
            dma((7, 2)), dma((7, 2)),
        ],
        compiler_params=pltpu.CompilerParams(collective_id=1, has_side_effects=True),
        name="halo",
    )(density, velocity, temper, fine)


def along_of(which, speed):
    along = None
    for dimen in range(3):
        sign = velocity_set[which][dimen]
        if sign == 1:
            along = speed[dimen] if along is None else along + speed[dimen]
        elif sign == -1:
            along = -speed[dimen] if along is None else along - speed[dimen]
    return along


def equilibrium(density, speed):
    square = 1.0 - 1.5 * (speed[0] * speed[0] + speed[1] * speed[1] + speed[2] * speed[2])
    weighted = {w: w * density for w in set(weight_flow)}
    rows_out = [weighted[weight_flow[0]] * square]
    for which in range(1, 19, 2):
        along = along_of(which, speed)
        rho = weighted[weight_flow[which]]
        even = rho * (square + 4.5 * along * along)
        odd = rho * (3.0 * along)
        rows_out += [even + odd, even - odd]
    return rows_out


def heat_equilibrium(temper, speed):
    rows_out = [weight_heat[0] * temper]
    for which in range(1, 7, 2):
        even = weight_heat[which] * temper
        odd = even * (4.0 * along_of(which, speed))
        rows_out += [even + odd, even - odd]
    return rows_out


def flow_moments(flow):
    density = flow[0]
    for which in range(1, 19):
        density = density + flow[which]
    inverse = 1.0 / density
    speed = []
    for dimen in range(3):
        total = None
        for which in range(19):
            sign = velocity_set[which][dimen]
            if sign == 1:
                total = flow[which] if total is None else total + flow[which]
            elif sign == -1:
                total = total - flow[which]
        speed.append(total * inverse)
    return density, speed


def collide(flow, heat, rate_flow, rate_heat):
    density, speed = flow_moments(flow)
    temper = functools.reduce(lambda a, b: a + b, heat)
    flow = [f - rate_flow * (f - e) for f, e in zip(flow, equilibrium(density, speed))]
    heat = [g - rate_heat * (g - e) for g, e in zip(heat, heat_equilibrium(temper, speed))]
    return flow, heat


def stream_plane(store, plane, values):
    height, width = values[0].shape
    for which, value in enumerate(values):
        off_x, off_y, off_z = stacked_set[which]
        if off_y:
            value = pltpu.roll(value, off_y % height, 0)
        if off_z:
            value = pltpu.roll(value, off_z % width, 1)
        store[which, plane + off_x + 1] = value


def fluid_kernel(fields, temp_out, vel_out, first, second):
    planes = fields.shape[1]
    size_x, size_y, size_z = temp_out.shape

    def one(plane, carry):
        density = fields[0, plane]
        speed = [fields[1, plane], fields[2, plane], fields[3, plane]]
        fine = fields[5, plane] == 1.0
        flow, heat = collide(
            equilibrium(density, speed),
            heat_equilibrium(fields[4, plane], speed),
            jnp.where(fine, 1.0 / 1.3, 1.0 / 0.9),
            jnp.where(fine, 1.0 / 1.1, 1.0 / 0.8),
        )
        stream_plane(first, plane, flow + heat)
        return carry

    def two(plane, carry):
        fine = fields[5, plane] == 1.0
        values = [first[which, plane + 1] for which in range(26)]
        flow, heat = collide(
            values[:19], values[19:], jnp.where(fine, 1.0 / 1.3, 0.0), jnp.where(fine, 1.0 / 1.1, 0.0)
        )
        stream_plane(second, plane, flow + heat)
        return carry

    def three(row, carry):
        plane = row + HALO + 1
        values = [second[which, plane, :size_y, :size_z] for which in range(26)]
        density, speed = flow_moments(values[:19])
        temp_out[row] = functools.reduce(lambda a, b: a + b, values[19:])
        for dimen in range(3):
            vel_out[dimen, row] = speed[dimen]
        return carry

    lax.fori_loop(0, planes, one, 0)
    lax.fori_loop(1, planes - 1, two, 0)
    lax.fori_loop(0, size_x, three, 0)


def run_fluid(fields, shape):
    planes, height, width = fields.shape[1:]
    whole = pl.BlockSpec(memory_space=VMEM)
    return pl.pallas_call(
        fluid_kernel,
        out_shape=(jax.ShapeDtypeStruct(shape, jnp.float32), jax.ShapeDtypeStruct((3,) + shape, jnp.float32)),
        in_specs=[whole],
        out_specs=(whole, whole),
        scratch_shapes=[VMEM((26, planes + 2, height, width), jnp.float32)] * 2,
        compiler_params=pltpu.CompilerParams(vmem_limit_bytes=52 * 1024 * 1024),
        name="fluid",
    )(fields)


def thirds(value):
    high = value.astype(jnp.bfloat16)
    rest = value - high.astype(jnp.float32)
    middle = rest.astype(jnp.bfloat16)
    low = (rest - middle.astype(jnp.float32)).astype(jnp.bfloat16)
    return [high, middle, low]


def one_hot(index, count):
    rows = lax.broadcasted_iota(jnp.int32, (count, index.shape[1]), 0)
    return rows == index


def take(table, index):
    rows, lanes = table.shape
    pick = one_hot(index // lanes, rows).astype(jnp.float32).astype(jnp.bfloat16)
    inside = one_hot(index % lanes, lanes)
    got = None
    for part in thirds(table):
        term = lax.dot_general(part, pick, (((0,), (0,)), ((), ())), preferred_element_type=jnp.float32)
        got = term if got is None else got + term
    return jnp.sum(jnp.where(inside, got, 0.0), axis=0, keepdims=True)


def put(values, index, rows, lanes):
    hot = one_hot(index // lanes, rows).astype(jnp.float32)
    inside = one_hot(index % lanes, lanes).astype(jnp.float32).astype(jnp.bfloat16)
    outs = []
    for value in values:
        total = None
        for part in thirds(value):
            left = (hot * part.astype(jnp.float32)).astype(jnp.bfloat16)
            term = lax.dot_general(left, inside, (((1,), (1,)), ((), ())), preferred_element_type=jnp.float32)
            total = term if total is None else total + term
        outs.append(total)
    return outs


def send_kernel(temp, cell, dest, coef, solid, temp_at, outgoing, slot):
    got = take(temp[...], cell[...])
    temp_at[...] = got
    groups, kinds, width = outgoing.shape
    span = temp.shape[1]
    named = one_hot(dest[...], groups).astype(jnp.float32)
    earlier = lax.broadcasted_iota(jnp.int32, (span, span), 0) < lax.broadcasted_iota(jnp.int32, (span, span), 1)
    earlier = earlier.astype(jnp.float32).astype(jnp.bfloat16)
    before = jnp.zeros((groups, 1), jnp.float32)
    ranks = []
    for start in range(0, named.shape[1], span):
        here = named[:, start : start + span]
        ahead = jnp.dot(here.astype(jnp.bfloat16), earlier, preferred_element_type=jnp.float32) + before
        ranks.append(jnp.sum(ahead * here, axis=0, keepdims=True))
        before = before + jnp.sum(here, axis=1, keepdims=True)
    slot[...] = dest[...] * width + jnp.concatenate(ranks, axis=1).astype(jnp.int32)
    filled = put([got, coef[...], solid[...]], slot[...], groups, width)
    for which in range(kinds):
        for group in range(groups):
            outgoing[group, which : which + 1, :] = filled[which][group : group + 1, :]


def local_call(kernel, outs, *args):
    whole = pl.BlockSpec(memory_space=VMEM)
    return pl.pallas_call(
        kernel,
        out_shape=tuple(jax.ShapeDtypeStruct(*o) for o in outs),
        in_specs=[whole] * len(args),
        out_specs=(whole,) * len(outs),
        name=kernel.__name__,
    )(*args)


def wall_kernel(
    sizes, outgoing, source, ambient, conduct, slot, cell, coef, temp_at, solid_out, flux_out,
    arrived, back, returned, residual, image, face_y, face_z, got_x, got_y, got_z, part, whole, held_x, held_g,
    own_sem, pair_send, pair_recv, back_send, back_recv, face_send, face_recv, x_send, x_recv, g_send, g_recv,
):
    count_x, count_y, count_z = sizes
    groups = count_y * count_z
    my_x, my_y, my_z = (lax.axis_index(axis) for axis in AXES)
    me = my_y * count_z + my_z
    mesh = pl.DeviceIdType.MESH
    size_x, size_y, size_z = source.shape

    def mate(step):
        other = lax.rem(me + step, groups)
        return (my_x, other // count_z, lax.rem(other, count_z))

    def row(step):
        return (lax.rem(my_x + step, count_x), my_y, my_z)

    def remote(src, dst, send, recv, device):
        return pltpu.make_async_remote_copy(
            src_ref=src, dst_ref=dst, send_sem=send, recv_sem=recv, device_id=device, device_id_type=mesh
        )

    barrier = pltpu.get_barrier_semaphore()
    for step in range(1, groups):
        pl.semaphore_signal(barrier, inc=1, device_id=mate(step), device_id_type=mesh)
    for step in range(1, count_x):
        pl.semaphore_signal(barrier, inc=1, device_id=row(step), device_id_type=mesh)
    pl.semaphore_wait(barrier, groups + count_x - 2)

    pairs = [
        remote(
            outgoing.at[lax.rem(me + step, groups)], arrived.at[step], pair_send.at[step], pair_recv.at[step], mate(step)
        )
        for step in range(1, groups)
    ]
    for copy in pairs:
        copy.start()
    own = pltpu.make_async_copy(outgoing.at[me], arrived.at[0], own_sem.at[0])
    own.start()

    y_next = (my_x, lax.rem(my_y + 1, count_y), my_z)
    y_last = (my_x, lax.rem(my_y + count_y - 1, count_y), my_z)
    z_next = (my_x, my_y, lax.rem(my_z + 1, count_z))
    z_last = (my_x, my_y, lax.rem(my_z + count_z - 1, count_z))

    def send_faces(which, field):
        value = field[...]
        face_y[which, 0] = value[:, 0, :]
        face_y[which, 1] = value[:, size_y - 1, :]
        turned = jnp.transpose(value.reshape(size_x * size_y, size_z))
        face_z[which, 0] = turned[0:8]
        face_z[which, 1] = turned[size_z - 8 : size_z]
        plan = (
            (field.at[size_x - 1], got_x.at[which, 0], row(1)),
            (field.at[0], got_x.at[which, 1], row(count_x - 1)),
            (face_y.at[which, 1], got_y.at[which, 0], y_next),
            (face_y.at[which, 0], got_y.at[which, 1], y_last),
            (face_z.at[which, 1], got_z.at[which, 0], z_next),
            (face_z.at[which, 0], got_z.at[which, 1], z_last),
        )
        copies = [
            remote(src, dst, face_send.at[which, at], face_recv.at[which, at], device)
            for at, (src, dst, device) in enumerate(plan)
        ]
        for copy in copies:
            copy.start()
        return copies

    def around(which, field, copies):
        for copy in copies:
            copy.wait()
        value = field[...]
        below_x = jnp.concatenate([got_x[which, 0][None], value[:-1]], axis=0)
        above_x = jnp.concatenate([value[1:], got_x[which, 1][None]], axis=0)
        at_y = lax.broadcasted_iota(jnp.int32, value.shape, 1)
        below_y = jnp.where(at_y == 0, got_y[which, 0][:, None, :], pltpu.roll(value, 1, 1))
        above_y = jnp.where(at_y == size_y - 1, got_y[which, 1][:, None, :], pltpu.roll(value, size_y - 1, 1))
        at_z = lax.broadcasted_iota(jnp.int32, value.shape, 2)

        def column(line):
            return jnp.transpose(jnp.broadcast_to(line, (size_z, size_x * size_y))).reshape(value.shape)

        below_z = jnp.where(at_z == 0, column(got_z[which, 0][7:8]), pltpu.roll(value, 1, 2))
        above_z = jnp.where(at_z == size_z - 1, column(got_z[which, 1][0:1]), pltpu.roll(value, size_z - 1, 2))
        return (above_x, below_x, above_y, below_y, above_z, below_z)

    conduct_copies = send_faces(0, conduct)
    conducts = around(0, conduct, conduct_copies)
    at_x, at_y, at_z = (lax.broadcasted_iota(jnp.int32, source.shape, dim) for dim in range(3))
    place_x, place_y, place_z = at_x + my_x * size_x, at_y + my_y * size_y, at_z + my_z * size_z
    inside = (
        place_x < count_x * size_x - 1, place_x > 0,
        place_y < count_y * size_y - 1, place_y > 0,
        place_z < count_z * size_z - 1, place_z > 0,
    )
    here = conduct[...]
    weights = [jnp.where(ok, 2.0 * here * other / (here + other), 0.0) for ok, other in zip(inside, conducts)]

    own.wait()
    for copy in pairs:
        copy.wait()
    landed = jnp.concatenate([arrived[step] for step in range(groups)], axis=1)
    solid_cell = (landed[2:3, :] + 0.5).astype(jnp.int32)
    gain, inflow = put([landed[1:2, :], landed[1:2, :] * landed[0:1, :]], solid_cell, size_x * size_y, size_z)
    residual[...] = source[...] + inflow.reshape(source.shape)
    diagonal = ambient[...] + gain.reshape(source.shape)

    def operate(which, field, copies):
        value = field[...]
        total = diagonal * value
        for weight, other in zip(weights, around(which, field, copies)):
            total = total + weight * (value - other)
        return total

    image[...] = operate(1, residual, send_faces(1, residual))
    twice = operate(2, image, send_faces(2, image))

    first, second = residual[...], image[...]
    products = [jnp.sum(jnp.sum(a * b, axis=0), axis=0, keepdims=True)
                for a, b in ((first, first), (first, second), (second, second), (second, twice))]
    part[...] = jnp.concatenate(products + products, axis=0)
    copies = [remote(part, held_x.at[step], x_send.at[step], x_recv.at[step], row(step)) for step in range(1, count_x)]
    for copy in copies:
        copy.start()
    total = part[...]
    for step, copy in enumerate(copies):
        copy.wait()
        total = total + held_x[step + 1]
    whole[...] = total
    copies = [remote(whole, held_g.at[step], g_send.at[step], g_recv.at[step], mate(step)) for step in range(1, groups)]
    for copy in copies:
        copy.start()
    for step, copy in enumerate(copies):
        copy.wait()
        total = total + held_g[step + 1]
    total = jnp.broadcast_to(jnp.sum(total, axis=1, keepdims=True), total.shape)
    norm, product, square, cross = (total[at : at + 1] for at in range(4))
    alpha = norm / product
    norm_next = norm - 2.0 * alpha * product + alpha * alpha * square
    product_next = product - 2.0 * alpha * square + alpha * alpha * cross
    ratio = norm_next / norm
    alpha_next = norm_next / (product_next - ratio * norm_next / alpha)
    on_first = alpha + alpha_next * (1.0 + ratio)
    on_second = alpha_next * alpha
    flat = (size_x * size_y, size_z)
    solid = on_first * first.reshape(flat) - on_second * second.reshape(flat)
    solid_out[...] = solid.reshape(source.shape)

    wall = take(solid, solid_cell)
    width = returned.shape[2]
    for step in range(groups):
        back[step] = wall[:, step * width : (step + 1) * width]
    copies = [
        remote(back.at[step], returned.at[me], back_send.at[step], back_recv.at[step], mate(groups - step))
        for step in range(1, groups)
    ]
    for copy in copies:
        copy.start()
    own = pltpu.make_async_copy(back.at[0], returned.at[me], own_sem.at[1])
    own.start()
    own.wait()
    for copy in copies:
        copy.wait()
    table = jnp.concatenate([returned[group] for group in range(groups)], axis=0)
    flux = coef[...] * (take(table, slot[...]) - temp_at[...])
    rows, lanes = flux_out.shape
    flux_out[...] = put([flux], cell[...], rows, lanes)[0]


def run_wall(fluid_flat, outgoing, source, *rest):
    sizes = tuple(lax.axis_size(axis) for axis in AXES)
    groups, kinds, width = outgoing.shape
    size_x, size_y, size_z = source.shape
    count_x = sizes[0]
    block = pl.BlockSpec(memory_space=VMEM)
    dma = pltpu.SemaphoreType.DMA

    def f32(*shape):
        return VMEM(shape, jnp.float32)

    return pl.pallas_call(
        functools.partial(wall_kernel, sizes),
        out_shape=(jax.ShapeDtypeStruct(source.shape, jnp.float32), jax.ShapeDtypeStruct(fluid_flat, jnp.float32)),
        in_specs=[block] * (2 + len(rest)),
        out_specs=(block, block),
        scratch_shapes=[
            f32(groups, kinds, width), f32(groups, 1, width), f32(groups, 1, width),
            f32(*source.shape), f32(*source.shape),
            f32(3, 2, size_x, size_z), f32(3, 2, 8, size_x * size_y),
            f32(3, 2, size_y, size_z), f32(3, 2, size_x, size_z), f32(3, 2, 8, size_x * size_y),
            f32(8, size_z), f32(8, size_z), f32(count_x, 8, size_z), f32(groups, 8, size_z),
            dma((2,)), dma((groups,)), dma((groups,)), dma((groups,)), dma((groups,)),
            dma((3, 6)), dma((3, 6)), dma((count_x,)), dma((count_x,)), dma((groups,)), dma((groups,)),
        ],
        compiler_params=pltpu.CompilerParams(collective_id=0, has_side_effects=True),
        name="wall",
    )(outgoing, source, *rest)


def per_device(
    density_start,
    velocity_start,
    temp_start,
    block_level,
    solid_source,
    ambient,
    conduct,
    pair_cell,
    pair_dest,
    pair_solid,
    pair_coef,
):
    size_x, size_y, size_z = density_start.shape
    blocks_x, blocks_y, blocks_z = block_level.shape
    fine = jnp.broadcast_to(
        (block_level == 1)[:, None, :, None, :, None], (blocks_x, BLK, blocks_y, BLK, blocks_z, BLK)
    ).reshape(size_x, size_y, size_z)
    fields = run_halo(density_start, velocity_start, temp_start, fine.astype(jnp.float32))
    fluid_temp, fluid_vel = run_fluid(fields, (size_x, size_y, size_z))

    groups = lax.axis_size(("gy", "gz"))
    pair_count = pair_cell.shape[0]
    capacity = 2 * pair_count // groups
    width = -(-capacity // size_z) * size_z
    dest = pair_dest.reshape(1, pair_count)
    cell = pair_cell[None, :]
    coef = pair_coef[None, :]
    solid = pair_solid.astype(jnp.float32)[None, :]
    flat = (size_x * size_y, size_z)
    temp_at, outgoing, slot = local_call(
        send_kernel,
        (((1, pair_count), jnp.float32), ((groups, 3, width), jnp.float32), ((1, pair_count), jnp.int32)),
        fluid_temp.reshape(flat), cell, dest, coef, solid,
    )
    solid_temp, wall_flux = run_wall(
        flat, outgoing, solid_source, ambient, conduct, slot, cell, coef, temp_at
    )
    return (fluid_temp, fluid_vel, solid_temp, wall_flux.reshape(size_x, size_y, size_z))


def solution(mesh):
    return jax.shard_map(
        per_device,
        mesh=mesh,
        in_specs=(
            P("gx", "gy", "gz"),
            P(None, "gx", "gy", "gz"),
            P("gx", "gy", "gz"),
            P("gx", "gy", "gz"),
            P("gx", "gy", "gz"),
            P("gx", "gy", "gz"),
            P("gx", "gy", "gz"),
            P(("gx", "gy", "gz")),
            P(("gx", "gy", "gz"), None),
            P(("gx", "gy", "gz")),
            P(("gx", "gy", "gz")),
        ),
        out_specs=(
            P("gx", "gy", "gz"),
            P(None, "gx", "gy", "gz"),
            P("gx", "gy", "gz"),
            P("gx", "gy", "gz"),
        ),
        check_vma=False,
    )
```

```python
import functools

import jax
import jax.numpy as jnp
from jax import lax
from jax.experimental import pallas as pl
from jax.experimental.pallas import tpu as pltpu
from jax.sharding import PartitionSpec as P

BLK = 16
ITERS = 2


velocity_set = (
    (0, 0, 0),
    (1, 0, 0),
    (-1, 0, 0),
    (0, 1, 0),
    (0, -1, 0),
    (0, 0, 1),
    (0, 0, -1),
    (1, 1, 0),
    (-1, -1, 0),
    (1, -1, 0),
    (-1, 1, 0),
    (1, 0, 1),
    (-1, 0, -1),
    (1, 0, -1),
    (-1, 0, 1),
    (0, 1, 1),
    (0, -1, -1),
    (0, 1, -1),
    (0, -1, 1),
)
weight_flow = (1.0 / 3.0,) + (1.0 / 18.0,) * 6 + (1.0 / 36.0,) * 12
weight_heat = (0.25,) + (0.125,) * 6
stacked_set = velocity_set + velocity_set[:7]


AXES = ("gx", "gy", "gz")
HALO = 2
VMEM = pltpu.VMEM


def halo_kernel(
    sizes, density, velocity, temper, fine, fields,
    got_x, pack_y, got_y, pack_c, got_c, pack_z, got_z, send_sem, recv_sem,
):
    size_x, size_y, size_z = density.shape
    kinds, planes = fields.shape[:2]
    spots = [lax.axis_index(axis) for axis in AXES]
    mesh = pl.DeviceIdType.MESH

    def beside(axis, step):
        moved = list(spots)
        moved[axis] = lax.rem(spots[axis] + (sizes[axis] + step), sizes[axis])
        return tuple(moved)

    barrier = pltpu.get_barrier_semaphore()
    for axis in range(3):
        for step in (1, -1):
            pl.semaphore_signal(barrier, inc=1, device_id=beside(axis, step), device_id_type=mesh)
    pl.semaphore_wait(barrier, 6)

    def both(number, axis, up, down, got):
        copies = [
            pltpu.make_async_remote_copy(
                src_ref=src, dst_ref=dst, send_sem=send_sem.at[number, side], recv_sem=recv_sem.at[number, side],
                device_id=beside(axis, step), device_id_type=mesh,
            )
            for side, (src, dst, step) in enumerate(((up, got[0], 1), (down, got[1], -1)))
            if side == 0 or sizes[axis] > 2 or up is not down
        ]
        for copy in copies:
            copy.start()
        return copies

    def finish(copies):
        for copy in copies:
            copy.wait()

    low, high = pl.ds(0, HALO), pl.ds(size_x - HALO, HALO)
    copies_x = []
    for number, (field, kind) in enumerate(((density, 0), (temper, 4), (fine, 5))):
        copies_x += both(number, 0, field.at[high], field.at[low], [got_x.at[side, kind] for side in range(2)])
    copies_x += both(
        3, 0, velocity.at[:, high], velocity.at[:, low], [got_x.at[side, pl.ds(1, 3)] for side in range(2)]
    )
    for kind, field in ((0, density), (4, temper), (5, fine)):
        fields[kind, HALO : HALO + size_x, :size_y, :size_z] = field[...]
    for kind in range(3):
        fields[kind + 1, HALO : HALO + size_x, :size_y, :size_z] = velocity[kind]

    row = lax.broadcasted_iota(jnp.int32, (8, size_z), 0)

    def packed(kind, plane):
        ends = [
            jnp.where(row < 4, fields[kind, at, 0:8, :size_z], fields[kind, at, size_y - 8 : size_y, :size_z])
            for at in (plane, plane + 1)
        ]
        return jnp.where(row < 4, pltpu.roll(ends[0], 2, 0), pltpu.roll(ends[1], 6, 0))

    def unpacked(kind, plane, below, above):
        mixed = jnp.where(row % 4 < 2, below, above)
        fields[kind, plane, size_y:, :size_z] = pltpu.roll(mixed, 6, 0)
        fields[kind, plane + 1, size_y:, :size_z] = pltpu.roll(mixed, 2, 0)

    for kind in range(kinds):
        for pair in range(size_x // 2):
            pack_y[kind, pair] = packed(kind, HALO + 2 * pair)
    copies_y = both(4, 1, pack_y, pack_y, [got_y.at[side] for side in range(2)])
    finish(copies_x)
    for kind in range(kinds):
        fields[kind, :HALO, :size_y, :size_z] = got_x[0, kind]
        fields[kind, HALO + size_x :, :size_y, :size_z] = got_x[1, kind]
    corners = (0, HALO + size_x)
    for kind in range(kinds):
        for corner, plane in enumerate(corners):
            pack_c[kind, corner] = packed(kind, plane)
    copies_c = both(5, 1, pack_c, pack_c, [got_c.at[side] for side in range(2)])
    next_y = len(copies_y) - 1
    finish(copies_y)
    for kind in range(kinds):
        for pair in range(size_x // 2):
            unpacked(kind, HALO + 2 * pair, got_y[0, kind, pair], got_y[next_y, kind, pair])
    finish(copies_c)
    for kind in range(kinds):
        for corner, plane in enumerate(corners):
            unpacked(kind, plane, got_c[0, kind, corner], got_c[next_y, kind, corner])

    per = size_z // 4
    lane = lax.broadcasted_iota(jnp.int32, (size_y + 8, size_z), 1)
    for group in range(pack_z.shape[0]):
        total = jnp.zeros((size_y + 8, size_z), jnp.float32)
        for spot in range(min(per, kinds * planes - group * per)):
            kind, plane = divmod(group * per + spot, planes)
            moved = pltpu.roll(fields[kind, plane, :, :size_z], (4 * spot + 2) % size_z, 1)
            total = jnp.where(lane // 4 == spot, moved, total)
        pack_z[group] = total
    copies = both(6, 2, pack_z, pack_z, [got_z.at[side] for side in range(2)])
    finish(copies)
    next_z = len(copies) - 1
    for group in range(pack_z.shape[0]):
        mixed = jnp.where(lane % 4 < 2, got_z[0, group], got_z[next_z, group])
        for spot in range(min(per, kinds * planes - group * per)):
            kind, plane = divmod(group * per + spot, planes)
            fields[kind, plane, :, size_z:] = pltpu.roll(mixed, (size_z - 4 * spot - 2) % size_z, 1)


def run_halo(density, velocity, temper, fine):
    sizes = tuple(lax.axis_size(axis) for axis in AXES)
    size_x, size_y, size_z = density.shape
    kinds = 6
    planes = size_x + 2 * HALO
    groups = -(-kinds * planes // (size_z // 4))
    block = pl.BlockSpec(memory_space=VMEM)
    dma = pltpu.SemaphoreType.DMA

    def f32(*shape):
        return VMEM(shape, jnp.float32)

    return pl.pallas_call(
        functools.partial(halo_kernel, sizes),
        out_shape=jax.ShapeDtypeStruct((kinds, planes, size_y + 8, 2 * size_z), jnp.float32),
        in_specs=[block] * 4,
        out_specs=block,
        scratch_shapes=[
            f32(2, kinds, HALO, size_y, size_z),
            f32(kinds, size_x // 2, 8, size_z), f32(2, kinds, size_x // 2, 8, size_z),
            f32(kinds, 2, 8, size_z), f32(2, kinds, 2, 8, size_z),
            f32(groups, size_y + 8, size_z), f32(2, groups, size_y + 8, size_z),
            dma((7, 2)), dma((7, 2)),
        ],
        compiler_params=pltpu.CompilerParams(collective_id=1, has_side_effects=True),
        name="halo",
    )(density, velocity, temper, fine)


def along_of(which, speed):
    along = None
    for dimen in range(3):
        sign = velocity_set[which][dimen]
        if sign == 1:
            along = speed[dimen] if along is None else along + speed[dimen]
        elif sign == -1:
            along = -speed[dimen] if along is None else along - speed[dimen]
    return along


def equilibrium(density, speed):
    square = 1.0 - 1.5 * (speed[0] * speed[0] + speed[1] * speed[1] + speed[2] * speed[2])
    weighted = {w: w * density for w in set(weight_flow)}
    rows_out = [weighted[weight_flow[0]] * square]
    for which in range(1, 19, 2):
        along = along_of(which, speed)
        rho = weighted[weight_flow[which]]
        even = rho * (square + 4.5 * along * along)
        odd = rho * (3.0 * along)
        rows_out += [even + odd, even - odd]
    return rows_out


def heat_equilibrium(temper, speed):
    rows_out = [weight_heat[0] * temper]
    for which in range(1, 7, 2):
        even = weight_heat[which] * temper
        odd = even * (4.0 * along_of(which, speed))
        rows_out += [even + odd, even - odd]
    return rows_out


def flow_moments(flow):
    density = flow[0]
    for which in range(1, 19):
        density = density + flow[which]
    inverse = 1.0 / density
    speed = []
    for dimen in range(3):
        total = None
        for which in range(19):
            sign = velocity_set[which][dimen]
            if sign == 1:
                total = flow[which] if total is None else total + flow[which]
            elif sign == -1:
                total = total - flow[which]
        speed.append(total * inverse)
    return density, speed


def collide(flow, heat, rate_flow, rate_heat):
    density, speed = flow_moments(flow)
    temper = functools.reduce(lambda a, b: a + b, heat)
    flow = [f - rate_flow * (f - e) for f, e in zip(flow, equilibrium(density, speed))]
    heat = [g - rate_heat * (g - e) for g, e in zip(heat, heat_equilibrium(temper, speed))]
    return flow, heat


def stream_plane(store, plane, values):
    height, width = values[0].shape
    for which, value in enumerate(values):
        off_x, off_y, off_z = stacked_set[which]
        if off_y:
            value = pltpu.roll(value, off_y % height, 0)
        if off_z:
            value = pltpu.roll(value, off_z % width, 1)
        store[which, plane + off_x + 1] = value


def fluid_kernel(fields, temp_out, vel_out, first, second):
    planes = fields.shape[1]
    size_x, size_y, size_z = temp_out.shape

    def one(plane, carry):
        density = fields[0, plane]
        speed = [fields[1, plane], fields[2, plane], fields[3, plane]]
        fine = fields[5, plane] == 1.0
        flow, heat = collide(
            equilibrium(density, speed),
            heat_equilibrium(fields[4, plane], speed),
            jnp.where(fine, 1.0 / 1.3, 1.0 / 0.9),
            jnp.where(fine, 1.0 / 1.1, 1.0 / 0.8),
        )
        stream_plane(first, plane, flow + heat)
        return carry

    def two(plane, carry):
        fine = fields[5, plane] == 1.0
        values = [first[which, plane + 1] for which in range(26)]
        flow, heat = collide(
            values[:19], values[19:], jnp.where(fine, 1.0 / 1.3, 0.0), jnp.where(fine, 1.0 / 1.1, 0.0)
        )
        stream_plane(second, plane, flow + heat)
        return carry

    def three(row, carry):
        plane = row + HALO + 1
        values = [second[which, plane, :size_y, :size_z] for which in range(26)]
        density, speed = flow_moments(values[:19])
        temp_out[row] = functools.reduce(lambda a, b: a + b, values[19:])
        for dimen in range(3):
            vel_out[dimen, row] = speed[dimen]
        return carry

    lax.fori_loop(0, planes, one, 0)
    lax.fori_loop(1, planes - 1, two, 0)
    lax.fori_loop(0, size_x, three, 0)


def run_fluid(fields, shape):
    planes, height, width = fields.shape[1:]
    whole = pl.BlockSpec(memory_space=VMEM)
    return pl.pallas_call(
        fluid_kernel,
        out_shape=(jax.ShapeDtypeStruct(shape, jnp.float32), jax.ShapeDtypeStruct((3,) + shape, jnp.float32)),
        in_specs=[whole],
        out_specs=(whole, whole),
        scratch_shapes=[VMEM((26, planes + 2, height, width), jnp.float32)] * 2,
        compiler_params=pltpu.CompilerParams(vmem_limit_bytes=52 * 1024 * 1024),
        name="fluid",
    )(fields)


def thirds(value):
    high = value.astype(jnp.bfloat16)
    rest = value - high.astype(jnp.float32)
    middle = rest.astype(jnp.bfloat16)
    low = (rest - middle.astype(jnp.float32)).astype(jnp.bfloat16)
    return [high, middle, low]


def one_hot(index, count):
    rows = lax.broadcasted_iota(jnp.int32, (count, index.shape[1]), 0)
    return rows == index


def take(table, index):
    rows, lanes = table.shape
    pick = one_hot(index // lanes, rows).astype(jnp.float32).astype(jnp.bfloat16)
    inside = one_hot(index % lanes, lanes)
    got = None
    for part in thirds(table):
        term = lax.dot_general(part, pick, (((0,), (0,)), ((), ())), preferred_element_type=jnp.float32)
        got = term if got is None else got + term
    return jnp.sum(jnp.where(inside, got, 0.0), axis=0, keepdims=True)


def put(values, index, rows, lanes):
    hot = one_hot(index // lanes, rows).astype(jnp.float32)
    inside = one_hot(index % lanes, lanes).astype(jnp.float32).astype(jnp.bfloat16)
    outs = []
    for value in values:
        total = None
        for part in thirds(value):
            left = (hot * part.astype(jnp.float32)).astype(jnp.bfloat16)
            term = lax.dot_general(left, inside, (((1,), (1,)), ((), ())), preferred_element_type=jnp.float32)
            total = term if total is None else total + term
        outs.append(total)
    return outs


def send_kernel(temp, cell, dest, coef, solid, temp_at, outgoing, slot):
    got = take(temp[...], cell[...])
    temp_at[...] = got
    groups, kinds, width = outgoing.shape
    span = temp.shape[1]
    named = one_hot(dest[...], groups).astype(jnp.float32)
    earlier = lax.broadcasted_iota(jnp.int32, (span, span), 0) < lax.broadcasted_iota(jnp.int32, (span, span), 1)
    earlier = earlier.astype(jnp.float32).astype(jnp.bfloat16)
    before = jnp.zeros((groups, 1), jnp.float32)
    ranks = []
    for start in range(0, named.shape[1], span):
        here = named[:, start : start + span]
        ahead = jnp.dot(here.astype(jnp.bfloat16), earlier, preferred_element_type=jnp.float32) + before
        ranks.append(jnp.sum(ahead * here, axis=0, keepdims=True))
        before = before + jnp.sum(here, axis=1, keepdims=True)
    slot[...] = dest[...] * width + jnp.concatenate(ranks, axis=1).astype(jnp.int32)
    filled = put([got, coef[...], solid[...].astype(jnp.float32)], slot[...], groups, width)
    for which in range(kinds):
        for group in range(groups):
            outgoing[group, which : which + 1, :] = filled[which][group : group + 1, :]


def local_call(kernel, outs, *args):
    whole = pl.BlockSpec(memory_space=VMEM)
    return pl.pallas_call(
        kernel,
        out_shape=tuple(jax.ShapeDtypeStruct(*o) for o in outs),
        in_specs=[whole] * len(args),
        out_specs=(whole,) * len(outs),
        name=kernel.__name__,
    )(*args)


def wall_kernel(
    sizes, outgoing, source, ambient, conduct, solid_out, returned_out,
    arrived, back, returned, residual, image, face_y, face_z, got_x, got_y, got_z, part, whole, held_x, held_g,
    own_sem, pair_send, pair_recv, back_send, back_recv, face_send, face_recv, x_send, x_recv, g_send, g_recv,
):
    count_x, count_y, count_z = sizes
    groups = count_y * count_z
    my_x, my_y, my_z = (lax.axis_index(axis) for axis in AXES)
    me = my_y * count_z + my_z
    mesh = pl.DeviceIdType.MESH
    size_x, size_y, size_z = source.shape

    def mate(step):
        other = lax.rem(me + step, groups)
        return (my_x, other // count_z, lax.rem(other, count_z))

    def row(step):
        return (lax.rem(my_x + step, count_x), my_y, my_z)

    def remote(src, dst, send, recv, device):
        return pltpu.make_async_remote_copy(
            src_ref=src, dst_ref=dst, send_sem=send, recv_sem=recv, device_id=device, device_id_type=mesh
        )

    barrier = pltpu.get_barrier_semaphore()
    for step in range(1, groups):
        pl.semaphore_signal(barrier, inc=1, device_id=mate(step), device_id_type=mesh)
    for step in range(1, count_x):
        pl.semaphore_signal(barrier, inc=1, device_id=row(step), device_id_type=mesh)
    pl.semaphore_wait(barrier, groups + count_x - 2)

    pairs = [
        remote(
            outgoing.at[lax.rem(me + step, groups)], arrived.at[step], pair_send.at[step], pair_recv.at[step], mate(step)
        )
        for step in range(1, groups)
    ]
    for copy in pairs:
        copy.start()
    own = pltpu.make_async_copy(outgoing.at[me], arrived.at[0], own_sem.at[0])
    own.start()

    y_next = (my_x, lax.rem(my_y + 1, count_y), my_z)
    y_last = (my_x, lax.rem(my_y + count_y - 1, count_y), my_z)
    z_next = (my_x, my_y, lax.rem(my_z + 1, count_z))
    z_last = (my_x, my_y, lax.rem(my_z + count_z - 1, count_z))

    def send_faces(which, field):
        plan = (
            (field.at[size_x - 1], got_x.at[which, 0], row(1)),
            (field.at[0], got_x.at[which, 1], row(count_x - 1)),
            (face_y.at[which, 1], got_y.at[which, 0], y_next),
            (face_y.at[which, 0], got_y.at[which, 1], y_last),
            (face_z.at[which, 1], got_z.at[which, 0], z_next),
            (face_z.at[which, 0], got_z.at[which, 1], z_last),
        )
        copies = [
            remote(src, dst, face_send.at[which, at], face_recv.at[which, at], device)
            for at, (src, dst, device) in enumerate(plan)
        ]
        copies[0].start()
        copies[1].start()
        value = field[...]
        face_y[which, 0] = value[:, 0, :]
        face_y[which, 1] = value[:, size_y - 1, :]
        turned = jnp.transpose(value.reshape(size_x * size_y, size_z))
        face_z[which, 0] = turned[0:8]
        face_z[which, 1] = turned[size_z - 8 : size_z]
        for copy in copies[2:]:
            copy.start()
        return copies

    def around(which, field, copies):
        for copy in copies:
            copy.wait()
        value = field[...]
        below_x = jnp.concatenate([got_x[which, 0][None], value[:-1]], axis=0)
        above_x = jnp.concatenate([value[1:], got_x[which, 1][None]], axis=0)
        at_y = lax.broadcasted_iota(jnp.int32, value.shape, 1)
        below_y = jnp.where(at_y == 0, got_y[which, 0][:, None, :], pltpu.roll(value, 1, 1))
        above_y = jnp.where(at_y == size_y - 1, got_y[which, 1][:, None, :], pltpu.roll(value, size_y - 1, 1))
        at_z = lax.broadcasted_iota(jnp.int32, value.shape, 2)

        def column(line):
            return jnp.transpose(jnp.broadcast_to(line, (size_z, size_x * size_y))).reshape(value.shape)

        below_z = jnp.where(at_z == 0, column(got_z[which, 0][7:8]), pltpu.roll(value, 1, 2))
        above_z = jnp.where(at_z == size_z - 1, column(got_z[which, 1][0:1]), pltpu.roll(value, size_z - 1, 2))
        return (above_x, below_x, above_y, below_y, above_z, below_z)

    conduct_copies = send_faces(0, conduct)
    own.wait()
    for copy in pairs:
        copy.wait()
    landed = jnp.concatenate([arrived[step] for step in range(groups)], axis=1)
    solid_cell = (landed[2:3, :] + 0.5).astype(jnp.int32)
    gain, inflow = put([landed[1:2, :], landed[1:2, :] * landed[0:1, :]], solid_cell, size_x * size_y, size_z)
    residual[...] = source[...] + inflow.reshape(source.shape)
    residual_copies = send_faces(1, residual)
    diagonal = ambient[...] + gain.reshape(source.shape)
    conducts = around(0, conduct, conduct_copies)
    at_x, at_y, at_z = (lax.broadcasted_iota(jnp.int32, source.shape, dim) for dim in range(3))
    place_x, place_y, place_z = at_x + my_x * size_x, at_y + my_y * size_y, at_z + my_z * size_z
    inside = (
        place_x < count_x * size_x - 1, place_x > 0,
        place_y < count_y * size_y - 1, place_y > 0,
        place_z < count_z * size_z - 1, place_z > 0,
    )
    here = conduct[...]
    weights = [jnp.where(ok, 2.0 * here * other / (here + other), 0.0) for ok, other in zip(inside, conducts)]

    def operate(which, field, copies):
        value = field[...]
        total = diagonal * value
        for weight, other in zip(weights, around(which, field, copies)):
            total = total + weight * (value - other)
        return total

    image[...] = operate(1, residual, residual_copies)
    twice = operate(2, image, send_faces(2, image))

    first, second = residual[...], image[...]
    products = [jnp.sum(jnp.sum(a * b, axis=0), axis=0, keepdims=True)
                for a, b in ((first, first), (first, second), (second, second), (second, twice))]
    part[...] = jnp.concatenate(products + products, axis=0)
    copies = [remote(part, held_x.at[step], x_send.at[step], x_recv.at[step], row(step)) for step in range(1, count_x)]
    for copy in copies:
        copy.start()
    total = part[...]
    for step, copy in enumerate(copies):
        copy.wait()
        total = total + held_x[step + 1]
    whole[...] = total
    copies = [remote(whole, held_g.at[step], g_send.at[step], g_recv.at[step], mate(step)) for step in range(1, groups)]
    for copy in copies:
        copy.start()
    for step, copy in enumerate(copies):
        copy.wait()
        total = total + held_g[step + 1]
    total = jnp.broadcast_to(jnp.sum(total, axis=1, keepdims=True), total.shape)
    norm, product, square, cross = (total[at : at + 1] for at in range(4))
    alpha = norm / product
    norm_next = norm - 2.0 * alpha * product + alpha * alpha * square
    product_next = product - 2.0 * alpha * square + alpha * alpha * cross
    ratio = norm_next / norm
    alpha_next = norm_next / (product_next - ratio * norm_next / alpha)
    on_first = alpha + alpha_next * (1.0 + ratio)
    on_second = alpha_next * alpha
    flat = (size_x * size_y, size_z)
    solid = on_first * first.reshape(flat) - on_second * second.reshape(flat)
    solid_out[...] = solid.reshape(source.shape)

    wall = take(solid, solid_cell)
    width = returned.shape[2]
    for step in range(groups):
        back[step] = wall[:, step * width : (step + 1) * width]
    copies = [
        remote(back.at[step], returned.at[me], back_send.at[step], back_recv.at[step], mate(groups - step))
        for step in range(1, groups)
    ]
    for copy in copies:
        copy.start()
    own = pltpu.make_async_copy(back.at[0], returned.at[me], own_sem.at[1])
    own.start()
    own.wait()
    for copy in copies:
        copy.wait()
    returned_out[...] = returned[...]


def flux_kernel(solid, returned, slot, cell, coef, temp_at, solid_out, flux_out):
    solid_out[...] = solid[...]
    table = jnp.concatenate([returned[group] for group in range(returned.shape[0])], axis=0)
    flux = coef[...] * (take(table, slot[...]) - temp_at[...])
    rows, lanes = flux_out.shape
    flux_out[...] = put([flux], cell[...], rows, lanes)[0]


def run_wall(outgoing, source, *rest):
    sizes = tuple(lax.axis_size(axis) for axis in AXES)
    groups, kinds, width = outgoing.shape
    size_x, size_y, size_z = source.shape
    count_x = sizes[0]
    block = pl.BlockSpec(memory_space=VMEM)
    dma = pltpu.SemaphoreType.DMA

    def f32(*shape):
        return VMEM(shape, jnp.float32)

    return pl.pallas_call(
        functools.partial(wall_kernel, sizes),
        out_shape=(jax.ShapeDtypeStruct(source.shape, jnp.float32), jax.ShapeDtypeStruct((groups, 1, width), jnp.float32)),
        in_specs=[block] * (2 + len(rest)),
        out_specs=(block, block),
        scratch_shapes=[
            f32(groups, kinds, width), f32(groups, 1, width), f32(groups, 1, width),
            f32(*source.shape), f32(*source.shape),
            f32(3, 2, size_x, size_z), f32(3, 2, 8, size_x * size_y),
            f32(3, 2, size_y, size_z), f32(3, 2, size_x, size_z), f32(3, 2, 8, size_x * size_y),
            f32(8, size_z), f32(8, size_z), f32(count_x, 8, size_z), f32(groups, 8, size_z),
            dma((2,)), dma((groups,)), dma((groups,)), dma((groups,)), dma((groups,)),
            dma((3, 6)), dma((3, 6)), dma((count_x,)), dma((count_x,)), dma((groups,)), dma((groups,)),
        ],
        compiler_params=pltpu.CompilerParams(collective_id=0, has_side_effects=True),
        name="wall",
    )(outgoing, source, *rest)


def per_device(
    density_start,
    velocity_start,
    temp_start,
    block_level,
    solid_source,
    ambient,
    conduct,
    pair_cell,
    pair_dest,
    pair_solid,
    pair_coef,
):
    size_x, size_y, size_z = density_start.shape
    blocks_x, blocks_y, blocks_z = block_level.shape
    fine = jnp.broadcast_to(
        (block_level == 1)[:, None, :, None, :, None], (blocks_x, BLK, blocks_y, BLK, blocks_z, BLK)
    ).reshape(size_x, size_y, size_z)
    fields = run_halo(density_start, velocity_start, temp_start, fine.astype(jnp.float32))
    fluid_temp, fluid_vel = run_fluid(fields, (size_x, size_y, size_z))

    groups = lax.axis_size(("gy", "gz"))
    pair_count = pair_cell.shape[0]
    capacity = 2 * pair_count // groups
    width = -(-capacity // size_z) * size_z
    dest = pair_dest.reshape(1, pair_count)
    cell = pair_cell[None, :]
    coef = pair_coef[None, :]
    solid = pair_solid[None, :]
    flat = (size_x * size_y, size_z)
    temp_at, outgoing, slot = local_call(
        send_kernel,
        (((1, pair_count), jnp.float32), ((groups, 3, width), jnp.float32), ((1, pair_count), jnp.int32)),
        fluid_temp.reshape(flat), cell, dest, coef, solid,
    )
    solid_temp, returned = run_wall(outgoing, solid_source, ambient, conduct)
    solid_temp, wall_flux = local_call(
        flux_kernel,
        ((solid_source.shape, jnp.float32), (flat, jnp.float32)),
        solid_temp, returned, slot, cell, coef, temp_at,
    )
    return (fluid_temp, fluid_vel, solid_temp, wall_flux.reshape(size_x, size_y, size_z))


def solution(mesh):
    return jax.shard_map(
        per_device,
        mesh=mesh,
        in_specs=(
            P("gx", "gy", "gz"),
            P(None, "gx", "gy", "gz"),
            P("gx", "gy", "gz"),
            P("gx", "gy", "gz"),
            P("gx", "gy", "gz"),
            P("gx", "gy", "gz"),
            P("gx", "gy", "gz"),
            P(("gx", "gy", "gz")),
            P(("gx", "gy", "gz"), None),
            P(("gx", "gy", "gz")),
            P(("gx", "gy", "gz")),
        ),
        out_specs=(
            P("gx", "gy", "gz"),
            P(None, "gx", "gy", "gz"),
            P("gx", "gy", "gz"),
            P("gx", "gy", "gz"),
        ),
        check_vma=False,
    )
```

```python
import functools

import jax
import jax.numpy as jnp
from jax import lax
from jax.experimental import pallas as pl
from jax.experimental.pallas import tpu as pltpu
from jax.sharding import PartitionSpec as P

BLK = 16
ITERS = 2


velocity_set = (
    (0, 0, 0),
    (1, 0, 0),
    (-1, 0, 0),
    (0, 1, 0),
    (0, -1, 0),
    (0, 0, 1),
    (0, 0, -1),
    (1, 1, 0),
    (-1, -1, 0),
    (1, -1, 0),
    (-1, 1, 0),
    (1, 0, 1),
    (-1, 0, -1),
    (1, 0, -1),
    (-1, 0, 1),
    (0, 1, 1),
    (0, -1, -1),
    (0, 1, -1),
    (0, -1, 1),
)
weight_flow = (1.0 / 3.0,) + (1.0 / 18.0,) * 6 + (1.0 / 36.0,) * 12
weight_heat = (0.25,) + (0.125,) * 6
stacked_set = velocity_set + velocity_set[:7]


AXES = ("gx", "gy", "gz")
HALO = 2
VMEM = pltpu.VMEM


def halo_kernel(
    sizes, density, velocity, temper, fine, fields,
    got_x, pack_y, got_y, pack_c, got_c, pack_z, got_z, send_sem, recv_sem,
):
    size_x, size_y, size_z = density.shape
    kinds, planes = fields.shape[:2]
    spots = [lax.axis_index(axis) for axis in AXES]
    mesh = pl.DeviceIdType.MESH

    def beside(axis, step):
        moved = list(spots)
        moved[axis] = lax.rem(spots[axis] + (sizes[axis] + step), sizes[axis])
        return tuple(moved)

    barrier = pltpu.get_barrier_semaphore()
    for axis in range(3):
        for step in (1, -1):
            pl.semaphore_signal(barrier, inc=1, device_id=beside(axis, step), device_id_type=mesh)
    pl.semaphore_wait(barrier, 6)

    def both(number, axis, up, down, got):
        copies = [
            pltpu.make_async_remote_copy(
                src_ref=src, dst_ref=dst, send_sem=send_sem.at[number, side], recv_sem=recv_sem.at[number, side],
                device_id=beside(axis, step), device_id_type=mesh,
            )
            for side, (src, dst, step) in enumerate(((up, got[0], 1), (down, got[1], -1)))
            if side == 0 or sizes[axis] > 2 or up is not down
        ]
        for copy in copies:
            copy.start()
        return copies

    def finish(copies):
        for copy in copies:
            copy.wait()

    low, high = pl.ds(0, HALO), pl.ds(size_x - HALO, HALO)
    copies_x = []
    for number, (field, kind) in enumerate(((density, 0), (temper, 4), (fine, 5))):
        copies_x += both(number, 0, field.at[high], field.at[low], [got_x.at[side, kind] for side in range(2)])
    copies_x += both(
        3, 0, velocity.at[:, high], velocity.at[:, low], [got_x.at[side, pl.ds(1, 3)] for side in range(2)]
    )
    for kind, field in ((0, density), (4, temper), (5, fine)):
        fields[kind, HALO : HALO + size_x, :size_y, :size_z] = field[...]
    for kind in range(3):
        fields[kind + 1, HALO : HALO + size_x, :size_y, :size_z] = velocity[kind]

    row = lax.broadcasted_iota(jnp.int32, (8, size_z), 0)

    def packed(kind, plane):
        ends = [
            jnp.where(row < 4, fields[kind, at, 0:8, :size_z], fields[kind, at, size_y - 8 : size_y, :size_z])
            for at in (plane, plane + 1)
        ]
        return jnp.where(row < 4, pltpu.roll(ends[0], 2, 0), pltpu.roll(ends[1], 6, 0))

    def unpacked(kind, plane, below, above):
        mixed = jnp.where(row % 4 < 2, below, above)
        fields[kind, plane, size_y:, :size_z] = pltpu.roll(mixed, 6, 0)
        fields[kind, plane + 1, size_y:, :size_z] = pltpu.roll(mixed, 2, 0)

    for kind in range(kinds):
        for pair in range(size_x // 2):
            pack_y[kind, pair] = packed(kind, HALO + 2 * pair)
    copies_y = both(4, 1, pack_y, pack_y, [got_y.at[side] for side in range(2)])
    finish(copies_x)
    for kind in range(kinds):
        fields[kind, :HALO, :size_y, :size_z] = got_x[0, kind]
        fields[kind, HALO + size_x :, :size_y, :size_z] = got_x[1, kind]
    corners = (0, HALO + size_x)
    for kind in range(kinds):
        for corner, plane in enumerate(corners):
            pack_c[kind, corner] = packed(kind, plane)
    copies_c = both(5, 1, pack_c, pack_c, [got_c.at[side] for side in range(2)])
    next_y = len(copies_y) - 1
    finish(copies_y)
    for kind in range(kinds):
        for pair in range(size_x // 2):
            unpacked(kind, HALO + 2 * pair, got_y[0, kind, pair], got_y[next_y, kind, pair])
    finish(copies_c)
    for kind in range(kinds):
        for corner, plane in enumerate(corners):
            unpacked(kind, plane, got_c[0, kind, corner], got_c[next_y, kind, corner])

    per = size_z // 4
    lane = lax.broadcasted_iota(jnp.int32, (size_y + 8, size_z), 1)
    for group in range(pack_z.shape[0]):
        total = jnp.zeros((size_y + 8, size_z), jnp.float32)
        for spot in range(min(per, kinds * planes - group * per)):
            kind, plane = divmod(group * per + spot, planes)
            moved = pltpu.roll(fields[kind, plane, :, :size_z], (4 * spot + 2) % size_z, 1)
            total = jnp.where(lane // 4 == spot, moved, total)
        pack_z[group] = total
    copies = both(6, 2, pack_z, pack_z, [got_z.at[side] for side in range(2)])
    finish(copies)
    next_z = len(copies) - 1
    for group in range(pack_z.shape[0]):
        mixed = jnp.where(lane % 4 < 2, got_z[0, group], got_z[next_z, group])
        for spot in range(min(per, kinds * planes - group * per)):
            kind, plane = divmod(group * per + spot, planes)
            fields[kind, plane, :, size_z:] = pltpu.roll(mixed, (size_z - 4 * spot - 2) % size_z, 1)


def run_halo(density, velocity, temper, fine):
    sizes = tuple(lax.axis_size(axis) for axis in AXES)
    size_x, size_y, size_z = density.shape
    kinds = 6
    planes = size_x + 2 * HALO
    groups = -(-kinds * planes // (size_z // 4))
    block = pl.BlockSpec(memory_space=VMEM)
    dma = pltpu.SemaphoreType.DMA

    def f32(*shape):
        return VMEM(shape, jnp.float32)

    return pl.pallas_call(
        functools.partial(halo_kernel, sizes),
        out_shape=jax.ShapeDtypeStruct((kinds, planes, size_y + 8, 2 * size_z), jnp.float32),
        in_specs=[block] * 4,
        out_specs=block,
        scratch_shapes=[
            f32(2, kinds, HALO, size_y, size_z),
            f32(kinds, size_x // 2, 8, size_z), f32(2, kinds, size_x // 2, 8, size_z),
            f32(kinds, 2, 8, size_z), f32(2, kinds, 2, 8, size_z),
            f32(groups, size_y + 8, size_z), f32(2, groups, size_y + 8, size_z),
            dma((7, 2)), dma((7, 2)),
        ],
        compiler_params=pltpu.CompilerParams(collective_id=1, has_side_effects=True),
        name="halo",
    )(density, velocity, temper, fine)


def along_of(which, speed):
    along = None
    for dimen in range(3):
        sign = velocity_set[which][dimen]
        if sign == 1:
            along = speed[dimen] if along is None else along + speed[dimen]
        elif sign == -1:
            along = -speed[dimen] if along is None else along - speed[dimen]
    return along


def equilibrium(density, speed):
    square = 1.0 - 1.5 * (speed[0] * speed[0] + speed[1] * speed[1] + speed[2] * speed[2])
    weighted = {w: w * density for w in set(weight_flow)}
    rows_out = [weighted[weight_flow[0]] * square]
    for which in range(1, 19, 2):
        along = along_of(which, speed)
        rho = weighted[weight_flow[which]]
        even = rho * (square + 4.5 * along * along)
        odd = rho * (3.0 * along)
        rows_out += [even + odd, even - odd]
    return rows_out


def heat_equilibrium(temper, speed):
    rows_out = [weight_heat[0] * temper]
    for which in range(1, 7, 2):
        even = weight_heat[which] * temper
        odd = even * (4.0 * along_of(which, speed))
        rows_out += [even + odd, even - odd]
    return rows_out


def flow_moments(flow):
    density = flow[0]
    for which in range(1, 19):
        density = density + flow[which]
    inverse = 1.0 / density
    speed = []
    for dimen in range(3):
        total = None
        for which in range(19):
            sign = velocity_set[which][dimen]
            if sign == 1:
                total = flow[which] if total is None else total + flow[which]
            elif sign == -1:
                total = total - flow[which]
        speed.append(total * inverse)
    return density, speed


def collide(flow, heat, rate_flow, rate_heat):
    density, speed = flow_moments(flow)
    temper = functools.reduce(lambda a, b: a + b, heat)
    flow = [f - rate_flow * (f - e) for f, e in zip(flow, equilibrium(density, speed))]
    heat = [g - rate_heat * (g - e) for g, e in zip(heat, heat_equilibrium(temper, speed))]
    return flow, heat


def stream_plane(store, plane, values):
    height, width = values[0].shape
    for which, value in enumerate(values):
        off_x, off_y, off_z = stacked_set[which]
        if off_y:
            value = pltpu.roll(value, off_y % height, 0)
        if off_z:
            value = pltpu.roll(value, off_z % width, 1)
        store[which, plane + off_x + 1] = value


def fluid_kernel(fields, temp_out, vel_out, first, second):
    planes = fields.shape[1]
    size_x, size_y, size_z = temp_out.shape

    def one(plane, carry):
        density = fields[0, plane]
        speed = [fields[1, plane], fields[2, plane], fields[3, plane]]
        fine = fields[5, plane] == 1.0
        flow, heat = collide(
            equilibrium(density, speed),
            heat_equilibrium(fields[4, plane], speed),
            jnp.where(fine, 1.0 / 1.3, 1.0 / 0.9),
            jnp.where(fine, 1.0 / 1.1, 1.0 / 0.8),
        )
        stream_plane(first, plane, flow + heat)
        return carry

    def two(plane, carry):
        fine = fields[5, plane] == 1.0
        values = [first[which, plane + 1] for which in range(26)]
        flow, heat = collide(
            values[:19], values[19:], jnp.where(fine, 1.0 / 1.3, 0.0), jnp.where(fine, 1.0 / 1.1, 0.0)
        )
        stream_plane(second, plane, flow + heat)
        return carry

    def three(row, carry):
        plane = row + HALO + 1
        values = [second[which, plane, :size_y, :size_z] for which in range(26)]
        density, speed = flow_moments(values[:19])
        temp_out[row] = functools.reduce(lambda a, b: a + b, values[19:])
        for dimen in range(3):
            vel_out[dimen, row] = speed[dimen]
        return carry

    lax.fori_loop(0, planes, one, 0)
    lax.fori_loop(1, planes - 1, two, 0)
    lax.fori_loop(0, size_x, three, 0)


def run_fluid(fields, shape):
    planes, height, width = fields.shape[1:]
    whole = pl.BlockSpec(memory_space=VMEM)
    return pl.pallas_call(
        fluid_kernel,
        out_shape=(jax.ShapeDtypeStruct(shape, jnp.float32), jax.ShapeDtypeStruct((3,) + shape, jnp.float32)),
        in_specs=[whole],
        out_specs=(whole, whole),
        scratch_shapes=[VMEM((26, planes + 2, height, width), jnp.float32)] * 2,
        compiler_params=pltpu.CompilerParams(vmem_limit_bytes=52 * 1024 * 1024),
        name="fluid",
    )(fields)


def thirds(value):
    high = value.astype(jnp.bfloat16)
    rest = value - high.astype(jnp.float32)
    middle = rest.astype(jnp.bfloat16)
    low = (rest - middle.astype(jnp.float32)).astype(jnp.bfloat16)
    return [high, middle, low]


def one_hot(index, count):
    rows = lax.broadcasted_iota(jnp.int32, (count, index.shape[1]), 0)
    return rows == index


def take(table, index):
    rows, lanes = table.shape
    pick = one_hot(index // lanes, rows).astype(jnp.float32).astype(jnp.bfloat16)
    inside = one_hot(index % lanes, lanes)
    got = None
    for part in thirds(table):
        term = lax.dot_general(part, pick, (((0,), (0,)), ((), ())), preferred_element_type=jnp.float32)
        got = term if got is None else got + term
    return jnp.sum(jnp.where(inside, got, 0.0), axis=0, keepdims=True)


def put(values, index, rows, lanes):
    hot = one_hot(index // lanes, rows).astype(jnp.float32).astype(jnp.bfloat16)
    inside = one_hot(index % lanes, lanes).astype(jnp.float32).astype(jnp.bfloat16)
    outs = []
    for value in values:
        total = None
        for part in thirds(value):
            left = hot * part
            term = lax.dot_general(left, inside, (((1,), (1,)), ((), ())), preferred_element_type=jnp.float32)
            total = term if total is None else total + term
        outs.append(total)
    return outs


def send_kernel(temp, cell, dest, coef, solid, temp_at, outgoing, slot):
    got = take(temp[...], cell[...])
    temp_at[...] = got
    groups, kinds, width = outgoing.shape
    span = temp.shape[1]
    named = one_hot(dest[...], groups).astype(jnp.float32)
    earlier = lax.broadcasted_iota(jnp.int32, (span, span), 0) < lax.broadcasted_iota(jnp.int32, (span, span), 1)
    earlier = earlier.astype(jnp.float32).astype(jnp.bfloat16)
    before = jnp.zeros((groups, 1), jnp.float32)
    ranks = []
    for start in range(0, named.shape[1], span):
        here = named[:, start : start + span]
        ahead = jnp.dot(here.astype(jnp.bfloat16), earlier, preferred_element_type=jnp.float32) + before
        ranks.append(jnp.sum(ahead * here, axis=0, keepdims=True))
        before = before + jnp.sum(here, axis=1, keepdims=True)
    slot[...] = dest[...] * width + jnp.concatenate(ranks, axis=1).astype(jnp.int32)
    filled = put([got, coef[...], solid[...].astype(jnp.float32)], slot[...], groups, width)
    for which in range(kinds):
        for group in range(groups):
            outgoing[group, which : which + 1, :] = filled[which][group : group + 1, :]


def local_call(kernel, outs, *args):
    whole = pl.BlockSpec(memory_space=VMEM)
    return pl.pallas_call(
        kernel,
        out_shape=tuple(jax.ShapeDtypeStruct(*o) for o in outs),
        in_specs=[whole] * len(args),
        out_specs=(whole,) * len(outs),
        name=kernel.__name__,
    )(*args)


def wall_kernel(
    sizes, outgoing, source, ambient, conduct, solid_out, returned_out,
    arrived, back, returned, residual, image, face_y, face_z, got_x, got_y, got_z, part, whole, held_x, held_g,
    own_sem, pair_send, pair_recv, back_send, back_recv, face_send, face_recv, x_send, x_recv, g_send, g_recv,
):
    count_x, count_y, count_z = sizes
    groups = count_y * count_z
    my_x, my_y, my_z = (lax.axis_index(axis) for axis in AXES)
    me = my_y * count_z + my_z
    mesh = pl.DeviceIdType.MESH
    size_x, size_y, size_z = source.shape

    def mate(step):
        other = lax.rem(me + step, groups)
        return (my_x, other // count_z, lax.rem(other, count_z))

    def row(step):
        return (lax.rem(my_x + step, count_x), my_y, my_z)

    def remote(src, dst, send, recv, device):
        return pltpu.make_async_remote_copy(
            src_ref=src, dst_ref=dst, send_sem=send, recv_sem=recv, device_id=device, device_id_type=mesh
        )

    barrier = pltpu.get_barrier_semaphore()
    for step in range(1, groups):
        pl.semaphore_signal(barrier, inc=1, device_id=mate(step), device_id_type=mesh)
    for step in range(1, count_x):
        pl.semaphore_signal(barrier, inc=1, device_id=row(step), device_id_type=mesh)
    pl.semaphore_wait(barrier, groups + count_x - 2)

    pairs = [
        remote(
            outgoing.at[lax.rem(me + step, groups)], arrived.at[step], pair_send.at[step], pair_recv.at[step], mate(step)
        )
        for step in range(1, groups)
    ]
    for copy in pairs:
        copy.start()
    own = pltpu.make_async_copy(outgoing.at[me], arrived.at[0], own_sem.at[0])
    own.start()

    y_next = (my_x, lax.rem(my_y + 1, count_y), my_z)
    y_last = (my_x, lax.rem(my_y + count_y - 1, count_y), my_z)
    z_next = (my_x, my_y, lax.rem(my_z + 1, count_z))
    z_last = (my_x, my_y, lax.rem(my_z + count_z - 1, count_z))

    def send_faces(which, field):
        plan = (
            (field.at[size_x - 1], got_x.at[which, 0], row(1)),
            (field.at[0], got_x.at[which, 1], row(count_x - 1)),
            (face_y.at[which, 1], got_y.at[which, 0], y_next),
            (face_y.at[which, 0], got_y.at[which, 1], y_last),
            (face_z.at[which, 1], got_z.at[which, 0], z_next),
            (face_z.at[which, 0], got_z.at[which, 1], z_last),
        )
        copies = [
            remote(src, dst, face_send.at[which, at], face_recv.at[which, at], device)
            for at, (src, dst, device) in enumerate(plan)
        ]
        copies[0].start()
        copies[1].start()
        value = field[...]
        face_y[which, 0] = value[:, 0, :]
        face_y[which, 1] = value[:, size_y - 1, :]
        turned = jnp.transpose(value.reshape(size_x * size_y, size_z))
        face_z[which, 0] = turned[0:8]
        face_z[which, 1] = turned[size_z - 8 : size_z]
        for copy in copies[2:]:
            copy.start()
        return copies

    def around(which, field, copies):
        for copy in copies:
            copy.wait()
        value = field[...]
        below_x = jnp.concatenate([got_x[which, 0][None], value[:-1]], axis=0)
        above_x = jnp.concatenate([value[1:], got_x[which, 1][None]], axis=0)
        at_y = lax.broadcasted_iota(jnp.int32, value.shape, 1)
        below_y = jnp.where(at_y == 0, got_y[which, 0][:, None, :], pltpu.roll(value, 1, 1))
        above_y = jnp.where(at_y == size_y - 1, got_y[which, 1][:, None, :], pltpu.roll(value, size_y - 1, 1))
        at_z = lax.broadcasted_iota(jnp.int32, value.shape, 2)

        def column(line):
            return jnp.transpose(jnp.broadcast_to(line, (size_z, size_x * size_y))).reshape(value.shape)

        below_z = jnp.where(at_z == 0, column(got_z[which, 0][7:8]), pltpu.roll(value, 1, 2))
        above_z = jnp.where(at_z == size_z - 1, column(got_z[which, 1][0:1]), pltpu.roll(value, size_z - 1, 2))
        return (above_x, below_x, above_y, below_y, above_z, below_z)

    conduct_copies = send_faces(0, conduct)
    own.wait()
    for copy in pairs:
        copy.wait()
    landed = jnp.concatenate([arrived[step] for step in range(groups)], axis=1)
    solid_cell = (landed[2:3, :] + 0.5).astype(jnp.int32)
    gain, inflow = put([landed[1:2, :], landed[1:2, :] * landed[0:1, :]], solid_cell, size_x * size_y, size_z)
    residual[...] = source[...] + inflow.reshape(source.shape)
    residual_copies = send_faces(1, residual)
    diagonal = ambient[...] + gain.reshape(source.shape)
    conducts = around(0, conduct, conduct_copies)
    at_x, at_y, at_z = (lax.broadcasted_iota(jnp.int32, source.shape, dim) for dim in range(3))
    place_x, place_y, place_z = at_x + my_x * size_x, at_y + my_y * size_y, at_z + my_z * size_z
    inside = (
        place_x < count_x * size_x - 1, place_x > 0,
        place_y < count_y * size_y - 1, place_y > 0,
        place_z < count_z * size_z - 1, place_z > 0,
    )
    here = conduct[...]
    weights = [jnp.where(ok, 2.0 * here * other / (here + other), 0.0) for ok, other in zip(inside, conducts)]

    def operate(which, field, copies):
        value = field[...]
        total = diagonal * value
        for weight, other in zip(weights, around(which, field, copies)):
            total = total + weight * (value - other)
        return total

    image[...] = operate(1, residual, residual_copies)
    twice = operate(2, image, send_faces(2, image))

    first, second = residual[...], image[...]
    products = [jnp.sum(jnp.sum(a * b, axis=0), axis=0, keepdims=True)
                for a, b in ((first, first), (first, second), (second, second), (second, twice))]
    part[...] = jnp.concatenate(products + products, axis=0)
    copies = [remote(part, held_x.at[step], x_send.at[step], x_recv.at[step], row(step)) for step in range(1, count_x)]
    for copy in copies:
        copy.start()
    total = part[...]
    for step, copy in enumerate(copies):
        copy.wait()
        total = total + held_x[step + 1]
    whole[...] = total
    copies = [remote(whole, held_g.at[step], g_send.at[step], g_recv.at[step], mate(step)) for step in range(1, groups)]
    for copy in copies:
        copy.start()
    for step, copy in enumerate(copies):
        copy.wait()
        total = total + held_g[step + 1]
    total = jnp.broadcast_to(jnp.sum(total, axis=1, keepdims=True), total.shape)
    norm, product, square, cross = (total[at : at + 1] for at in range(4))
    alpha = norm / product
    norm_next = norm - 2.0 * alpha * product + alpha * alpha * square
    product_next = product - 2.0 * alpha * square + alpha * alpha * cross
    ratio = norm_next / norm
    alpha_next = norm_next / (product_next - ratio * norm_next / alpha)
    on_first = alpha + alpha_next * (1.0 + ratio)
    on_second = alpha_next * alpha
    flat = (size_x * size_y, size_z)
    solid = on_first * first.reshape(flat) - on_second * second.reshape(flat)
    solid_out[...] = solid.reshape(source.shape)

    wall = take(solid, solid_cell)
    width = returned.shape[2]
    for step in range(groups):
        back[step] = wall[:, step * width : (step + 1) * width]
    copies = [
        remote(back.at[step], returned.at[me], back_send.at[step], back_recv.at[step], mate(groups - step))
        for step in range(1, groups)
    ]
    for copy in copies:
        copy.start()
    own = pltpu.make_async_copy(back.at[0], returned.at[me], own_sem.at[1])
    own.start()
    own.wait()
    for copy in copies:
        copy.wait()
    returned_out[...] = returned[...]


def flux_kernel(solid, returned, slot, cell, coef, temp_at, solid_out, flux_out):
    solid_out[...] = solid[...]
    table = jnp.concatenate([returned[group] for group in range(returned.shape[0])], axis=0)
    flux = coef[...] * (take(table, slot[...]) - temp_at[...])
    rows, lanes = flux_out.shape
    flux_out[...] = put([flux], cell[...], rows, lanes)[0]


def run_wall(outgoing, source, *rest):
    sizes = tuple(lax.axis_size(axis) for axis in AXES)
    groups, kinds, width = outgoing.shape
    size_x, size_y, size_z = source.shape
    count_x = sizes[0]
    block = pl.BlockSpec(memory_space=VMEM)
    dma = pltpu.SemaphoreType.DMA

    def f32(*shape):
        return VMEM(shape, jnp.float32)

    return pl.pallas_call(
        functools.partial(wall_kernel, sizes),
        out_shape=(jax.ShapeDtypeStruct(source.shape, jnp.float32), jax.ShapeDtypeStruct((groups, 1, width), jnp.float32)),
        in_specs=[block] * (2 + len(rest)),
        out_specs=(block, block),
        scratch_shapes=[
            f32(groups, kinds, width), f32(groups, 1, width), f32(groups, 1, width),
            f32(*source.shape), f32(*source.shape),
            f32(3, 2, size_x, size_z), f32(3, 2, 8, size_x * size_y),
            f32(3, 2, size_y, size_z), f32(3, 2, size_x, size_z), f32(3, 2, 8, size_x * size_y),
            f32(8, size_z), f32(8, size_z), f32(count_x, 8, size_z), f32(groups, 8, size_z),
            dma((2,)), dma((groups,)), dma((groups,)), dma((groups,)), dma((groups,)),
            dma((3, 6)), dma((3, 6)), dma((count_x,)), dma((count_x,)), dma((groups,)), dma((groups,)),
        ],
        compiler_params=pltpu.CompilerParams(collective_id=0, has_side_effects=True),
        name="wall",
    )(outgoing, source, *rest)


def per_device(
    density_start,
    velocity_start,
    temp_start,
    block_level,
    solid_source,
    ambient,
    conduct,
    pair_cell,
    pair_dest,
    pair_solid,
    pair_coef,
):
    size_x, size_y, size_z = density_start.shape
    blocks_x, blocks_y, blocks_z = block_level.shape
    fine = jnp.broadcast_to(
        (block_level == 1)[:, None, :, None, :, None], (blocks_x, BLK, blocks_y, BLK, blocks_z, BLK)
    ).reshape(size_x, size_y, size_z)
    fields = run_halo(density_start, velocity_start, temp_start, fine.astype(jnp.float32))
    fluid_temp, fluid_vel = run_fluid(fields, (size_x, size_y, size_z))

    groups = lax.axis_size(("gy", "gz"))
    pair_count = pair_cell.shape[0]
    capacity = 2 * pair_count // groups
    width = -(-capacity // size_z) * size_z
    dest = pair_dest.reshape(1, pair_count)
    cell = pair_cell[None, :]
    coef = pair_coef[None, :]
    solid = pair_solid[None, :]
    flat = (size_x * size_y, size_z)
    temp_at, outgoing, slot = local_call(
        send_kernel,
        (((1, pair_count), jnp.float32), ((groups, 3, width), jnp.float32), ((1, pair_count), jnp.int32)),
        fluid_temp.reshape(flat), cell, dest, coef, solid,
    )
    solid_temp, returned = run_wall(outgoing, solid_source, ambient, conduct)
    solid_temp, wall_flux = local_call(
        flux_kernel,
        ((solid_source.shape, jnp.float32), (flat, jnp.float32)),
        solid_temp, returned, slot, cell, coef, temp_at,
    )
    return (fluid_temp, fluid_vel, solid_temp, wall_flux.reshape(size_x, size_y, size_z))


def solution(mesh):
    return jax.shard_map(
        per_device,
        mesh=mesh,
        in_specs=(
            P("gx", "gy", "gz"),
            P(None, "gx", "gy", "gz"),
            P("gx", "gy", "gz"),
            P("gx", "gy", "gz"),
            P("gx", "gy", "gz"),
            P("gx", "gy", "gz"),
            P("gx", "gy", "gz"),
            P(("gx", "gy", "gz")),
            P(("gx", "gy", "gz"), None),
            P(("gx", "gy", "gz")),
            P(("gx", "gy", "gz")),
        ),
        out_specs=(
            P("gx", "gy", "gz"),
            P(None, "gx", "gy", "gz"),
            P("gx", "gy", "gz"),
            P("gx", "gy", "gz"),
        ),
        check_vma=False,
    )
```
